128 devices in a mesh: gx: 16 (over x, z), gy: 8 (over y, core).
Axes of the slice: x: 4, y: 4, z: 4, core: 2. Of those that a mesh axis runs over, the one named last changes fastest.
Arguments:
- velocity: float32 [3, 512, 512, 128], P(None, 'gx', 'gy'), may hold values from -6 to 6
- forces: float32 [16384, 3, 256], P(('gx', 'gy')), may hold values from -48 to 48
- offsets: float32 [16384, 3, 256], P(('gx', 'gy')), may hold values from 0 to 1
- base_x: int32 [16384, 256], P(('gx', 'gy')), may hold values from 0 to 12
- base_y: int32 [16384, 256], P(('gx', 'gy')), may hold values from 0 to 4
- base_z: int32 [16384, 256], P(('gx', 'gy')), may hold values from 0 to 124
- home_device: int32 [16384, 1], P(('gx', 'gy')), may hold values from 0 to 127; in each aligned block of 128 rows (0 to 127, 128 to 255, ...) at most 2 rows name the same one
- home_tile: int32 [16384], P(('gx', 'gy')), may hold values from 0 to 15
Outputs:
- velocity_next: float32 [3, 512, 512, 128], P(None, 'gx', 'gy')
- fibre_velocity: float32 [16384, 3, 256], P(('gx', 'gy'))
The draws below stay inside these ranges and needn't reach their ends.
Inputs may be any that keep to these rules, and one draw needn't show every extreme that they name: `home_device`: among the 128 blocks of one device no home device is named more than 2 times, and in every draw some device names some home exactly 2 times.
All inputs are finite; a program needn't handle non-finite values.
Results may differ from the reference program's by a relative error of at most 0.0035.
Values sent between devices are 32-bit elements; how exact they have to be, the bound alone decides.
No kernel may reach another device: no remote copies, remote signals or barrier semaphores. Data moves between devices by JAX's collectives and lax.ppermute only.
A program may use at most 64 MiB of HBM per device.

```python
import math
import jax
import jax.numpy as jnp
import numpy as np
from jax import lax

CX = 32
CY = 64
CZ = 128
BLK_DEV = 128
TX = 16
TY = 8
PTS = 256
NX = 512
NY = 512
BLOCKS = 16384
CAP = 2
N_GX = 16
N_GY = 8


def place_ends(drawn, stream_key, low, top_value):
    dims = drawn.shape
    index_at = [jax.random.randint(jax.random.fold_in(stream_key, axis), (), 0, dims[axis]) for axis in range(len(dims))]
    drawn = drawn.at[tuple(index_at)].set(low)
    longest = dims.index(max(dims))
    index_at[longest] = (index_at[longest] + 1) % dims[longest]
    return drawn.at[tuple(index_at)].set(top_value)


def block_scale(rng, dims, cuts, smallest, largest):
    def one(dim, blocks):
        heights = jax.random.uniform(jax.random.fold_in(jax.random.fold_in(rng, 6), dim), (blocks,), jnp.float32, smallest / len(cuts), largest / len(cuts))
        return jnp.repeat(jnp.exp(heights), dims[dim] // blocks).reshape((-1,) + (1,) * (len(dims) - dim - 1))

    loudness = one(*cuts[0])
    for cut in cuts[1:]:
        loudness = loudness * one(*cut)
    return loudness


def routed_block(key, own, number, rows, number_of, top, bound, skew):
    order = jax.random.permutation(key, number_of)
    crowded, usual = load_shares(number_of, rows * top, bound, skew, True), load_shares(number_of, rows * top, bound, skew, False)
    places = jnp.arange(number_of)

    def named(sizes, offset_by):
        used = int((sizes > 0).sum())
        fixed = max(1, used // 4)
        shifted = fixed + (places - fixed + offset_by * (used - fixed)) % max(1, number_of - fixed)
        return jnp.zeros((number_of,), jnp.int32).at[order[jnp.where(places < fixed, places, shifted)]].set(jnp.asarray(sizes, jnp.int32))

    sizes = jnp.where(number % 4 == 0, named(crowded, number // 4), named(usual, number - number // 4 - 1))
    mixed = jax.random.permutation(jax.random.fold_in(own, 3), number_of)
    source_of, taker = mixed[0:number_of // 2 * 2:2], mixed[1:number_of // 2 * 2:2]
    slack = jnp.minimum(sizes[source_of] - 1, bound - sizes[taker]) // 2
    slack = jnp.where((source_of == order[0]) | (taker == order[0]) | (sizes[taker] == 0), 0, jnp.maximum(slack, 0))
    shifted = jax.random.randint(jax.random.fold_in(own, 4), (number_of // 2,), 0, 1 << 20) % (slack + 1)
    sizes = sizes.at[source_of].add(-shifted).at[taker].add(shifted)
    members = jnp.searchsorted(jnp.cumsum(sizes), jnp.arange(rows * top), side="right").astype(jnp.int32)
    table = members.reshape(top, rows).T
    table = table[jax.random.permutation(jax.random.fold_in(own, 1), rows)]
    offset_by = jax.random.randint(jax.random.fold_in(own, 2), (rows, 1), 0, top)
    return jnp.take_along_axis(table, (jnp.arange(top)[None, :] + offset_by) % top, axis=1)


def load_shares(count, total, reach, lean, full):
    loads = [(1 << 20) // math.isqrt(rank ** lean) + 1 for rank in range(1, count + 1)]
    largest = reach if full else min(reach, max(-(-total // count), total * loads[0] // sum(loads)))
    least = 1 if total - largest >= count - 1 else 0
    holding, surplus = [largest] + [least] * (count - 1), total - largest - least * (count - 1)
    while surplus > 0:
        movable = [i for i in range(1, count) if holding[i] < largest] or [i for i in range(1, count) if holding[i] < reach]
        mass, remaining = sum([loads[i] for i in movable]), surplus
        for i in movable:
            extra = min(reach - holding[i], max(1, remaining * loads[i] // mass), surplus)
            holding[i] = holding[i] + extra
            surplus = surplus - extra
    return np.array(holding)


def noise(key, shape, deviation, bound, cuts=(), kind=jnp.bfloat16):
    array = jax.random.normal(key, shape, jnp.float32) * deviation
    if len(cuts) > 0:
        array = block_scale(key, shape, cuts, -0.22, 0.18) * array
    return jnp.clip(array, min=-bound, max=bound).astype(kind)


def setup_inputs(seed: int = 0) -> dict:
    arg_keys = jax.random.split(jax.random.key(seed), 9)
    velocity = noise(arg_keys[0], (3, NX, NY, CZ), 1.0, 6.0, ((1, 16), (2, 8)), jnp.float32)
    forces = noise(arg_keys[1], (BLOCKS, 3, PTS), 8.0, 48.0, ((0, 128),), jnp.float32)
    offsets = jnp.clip(1.0 * jax.random.uniform(arg_keys[2], (BLOCKS, 3, PTS), jnp.float32) ** block_scale(arg_keys[2], (BLOCKS, 3, PTS), ((0, 128),), -0.2, 0.2), 0.0, 1.0)
    base_x = place_ends(jax.random.randint(arg_keys[3], (BLOCKS, PTS), 0, TX - 3), jax.random.fold_in(arg_keys[3], 1), 0, (TX - 3) - 1).astype(jnp.int32)
    base_y = place_ends(jax.random.randint(arg_keys[4], (BLOCKS, PTS), 0, TY - 3), jax.random.fold_in(arg_keys[4], 1), 0, (TY - 3) - 1).astype(jnp.int32)
    base_z = place_ends(jax.random.randint(arg_keys[5], (BLOCKS, PTS), 0, CZ - 3), jax.random.fold_in(arg_keys[5], 1), 0, (CZ - 3) - 1).astype(jnp.int32)
    home_device_keys = jax.random.split(jax.random.fold_in(arg_keys[6], 1), BLOCKS // BLK_DEV)
    home_device_turns = jax.random.permutation(jax.random.fold_in(arg_keys[6], 3), BLOCKS // BLK_DEV)
    home_device = jax.vmap(lambda own, number: routed_block(jax.random.fold_in(arg_keys[6], 2), own, number, BLK_DEV, N_GX * N_GY, 1, CAP, 2))(home_device_keys, home_device_turns).reshape((BLOCKS, 1))
    home_tile = place_ends(jax.random.randint(arg_keys[7], (BLOCKS,), 0, (CX // TX) * (CY // TY)), jax.random.fold_in(arg_keys[7], 1), 0, ((CX // TX) * (CY // TY)) - 1).astype(jnp.int32)
    return {"velocity": velocity, "forces": forces, "offsets": offsets, "base_x": base_x, "base_y": base_y, "base_z": base_z, "home_device": home_device, "home_tile": home_tile}


time_step = 0.4
viscosity = 0.15

def peskin_weights(offset):
    radical = jnp.sqrt(1.0 + 4.0 * offset - 4.0 * offset * offset)
    return ((3.0 - 2.0 * offset - radical) / 8.0, (3.0 - 2.0 * offset + radical) / 8.0, (1.0 + 2.0 * offset + radical) / 8.0, (1.0 + 2.0 * offset - radical) / 8.0)

def dense_factor(corner, offset, length):
    cell_ids = jnp.arange(length, dtype=jnp.int32)
    running = jnp.zeros(offset.shape + (length,), offset.dtype)
    for shift_amount, weight in enumerate(peskin_weights(offset)):
        running = running + jnp.where(cell_ids == corner[..., None] + shift_amount, weight[..., None], 0.0)
    return running

def block_factors(floats_g, index_g, depth_cells):
    along_x = dense_factor(index_g[:, 0], floats_g[:, 3], TX)
    along_y = dense_factor(index_g[:, 1], floats_g[:, 4], TY)
    along_z = dense_factor(index_g[:, 2], floats_g[:, 5], depth_cells)
    group_size, points = (along_x.shape[0], along_x.shape[1])
    kernel_xy = (along_x[:, :, :, None] * along_y[:, :, None, :]).reshape(group_size, points, TX * TY).astype(jnp.bfloat16)
    return (kernel_xy, along_z)

def tiles_to_field(tile_data, count_x, count_y, depth_cells):
    shaped = tile_data.reshape(count_x, count_y, TX, TY, 3, depth_cells)
    return jnp.transpose(shaped, (4, 0, 2, 1, 3, 5)).reshape(3, count_x * TX, count_y * TY, depth_cells)

def field_to_tiles(field, count_x, count_y):
    depth_cells = field.shape[3]
    shaped = field.reshape(3, count_x, TX, count_y, TY, depth_cells)
    return jnp.transpose(shaped, (1, 3, 2, 4, 0, 5)).reshape(count_x * count_y, TX * TY, 3 * depth_cells)

def fluid_sweep(padded):
    boxed = jnp.pad(padded, ((0, 0), (0, 0), (0, 0), (1, 1)))
    centre = boxed[:, 1:-1, 1:-1, 1:-1]
    plus_x = boxed[:, 2:, 1:-1, 1:-1]
    minus_x = boxed[:, :-2, 1:-1, 1:-1]
    plus_y = boxed[:, 1:-1, 2:, 1:-1]
    minus_y = boxed[:, 1:-1, :-2, 1:-1]
    plus_z = boxed[:, 1:-1, 1:-1, 2:]
    minus_z = boxed[:, 1:-1, 1:-1, :-2]
    laplace = plus_x + minus_x + plus_y + minus_y + plus_z + minus_z - 6.0 * centre
    advect = (centre[0:1] * (plus_x - minus_x) + centre[1:2] * (plus_y - minus_y) + centre[2:3] * (plus_z - minus_z)) * 0.5
    return centre + time_step * (viscosity * laplace - advect)

def reference(velocity, forces, offsets, base_x, base_y, base_z, home_device, home_tile):
    points = forces.shape[2]
    depth_cells = velocity.shape[3]
    tiles_x = CX // TX
    tiles_y = CY // TY
    count_x = N_GX * tiles_x
    count_y = N_GY * tiles_y
    target = home_device[:, 0]
    global_x = target // N_GY * tiles_x + home_tile // tiles_y
    global_y = target % N_GY * tiles_y + home_tile % tiles_y
    global_tile = (global_x * count_y + global_y).astype(jnp.int32)
    payload = jnp.concatenate([forces, offsets], axis=1).reshape(-1, BLK_DEV, 6, points)
    indices = jnp.stack([base_x, base_y, base_z], axis=1).reshape(-1, BLK_DEV, 3, points)
    tile_groups = global_tile.reshape(-1, BLK_DEV)

    def spread_group(force_tiles, group_items):
        floats_g, index_g, tile_g = group_items
        kernel_xy, along_z = block_factors(floats_g, index_g, depth_cells)
        weighted = jnp.transpose(floats_g[:, 0:3], (0, 2, 1))[:, :, :, None] * along_z[:, :, None, :]
        weighted = weighted.reshape(BLK_DEV, points, 3 * depth_cells).astype(jnp.bfloat16)
        pieces = jnp.einsum('gpa,gpb->gab', kernel_xy.astype(jnp.float32), weighted.astype(jnp.float32), precision=lax.Precision.HIGHEST)
        return (force_tiles.at[tile_g].add(pieces), None)
    start = jnp.zeros((count_x * count_y, TX * TY, 3 * depth_cells), jnp.float32)
    force_tiles, _ = lax.scan(spread_group, start, (payload, indices, tile_groups))
    force_field = tiles_to_field(force_tiles, count_x, count_y, depth_cells)
    forced = velocity + time_step * force_field
    padded = jnp.pad(forced, ((0, 0), (1, 1), (1, 1), (0, 0)))
    velocity_next = fluid_sweep(padded)
    tiled = field_to_tiles(velocity_next, count_x, count_y).astype(jnp.bfloat16)

    def interpolate_group(carry, group_items):
        floats_g, index_g, tile_g = group_items
        kernel_xy, along_z = block_factors(floats_g, index_g, depth_cells)
        fetched = tiled[tile_g]
        hidden = jnp.einsum('gpa,gab->gpb', kernel_xy.astype(jnp.float32), fetched.astype(jnp.float32), precision=lax.Precision.HIGHEST)
        hidden = hidden.reshape(BLK_DEV, points, 3, depth_cells)
        result = lax.optimization_barrier(jnp.sum(hidden * along_z[:, :, None, :], axis=3))
        return (carry, jnp.transpose(result, (0, 2, 1)))
    _, replies = lax.scan(interpolate_group, jnp.zeros((), jnp.float32), (payload, indices, tile_groups))
    fibre_velocity = replies.reshape(-1, 3, points)
    return (velocity_next, fibre_velocity)
```

```python
import jax
import jax.numpy as jnp
from jax import lax
from jax.experimental import pallas as pl
from jax.experimental.pallas import tpu as pltpu
from jax.sharding import PartitionSpec as P

TX = 16
TY = 8
ROWS = 40
AXES = ("gx", "gy")

time_step = 0.4
viscosity = 0.15


def force_row(rank, idx):
    k, odd = idx // 2, idx % 2
    return jnp.where(rank == 0, 16 + idx, (6, 30, 38)[k] + odd)


def pack_kernel(home_ref, tile_ref, forces_ref, offsets_ref, bx_ref, by_ref, bz_ref, send_ref, slot_ref, count_ref):
    blocks = forces_ref.shape[1]
    devices = send_ref.shape[0] // ROWS

    def clear(d, carry):
        count_ref[d] = 0
        send_ref[pl.ds(d * ROWS + 14, 2), :] = jnp.full((2, 128), -1.0, jnp.float32)
        return carry

    lax.fori_loop(0, devices, clear, 0, unroll=8)

    def place(group, carry):
        b0 = pl.multiple_of(group * 8, 8)
        rows, marks = [], []
        for j in range(8):
            home = home_ref[b0 + j]
            rank = count_ref[home]
            count_ref[home] = rank + 1
            slot_ref[b0 + j] = home * 2 + rank
            rows.append((home * ROWS, rank))
            marks.append(tile_ref[b0 + j].astype(jnp.float32))
        for q in range(2):
            lanes = slice(q * 128, (q + 1) * 128)
            for v in range(3):
                idx = q * 3 + v
                off = offsets_ref[v, pl.ds(b0, 8), lanes]
                base = (bx_ref, by_ref, bz_ref)[v][pl.ds(b0, 8), lanes].astype(jnp.float32)
                force = forces_ref[v, pl.ds(b0, 8), lanes]
                for j, (row0, rank) in enumerate(rows):
                    send_ref[pl.ds(row0 + 24 * rank + idx, 1), :] = off[j : j + 1, :]
                    send_ref[pl.ds(row0 + 24 * rank + 8 + idx, 1), :] = base[j : j + 1, :]
                    send_ref[pl.ds(row0 + force_row(rank, idx), 1), :] = force[j : j + 1, :]
        for j, (row0, rank) in enumerate(rows):
            send_ref[pl.ds(row0 + 14 + rank, 1), :] = jnp.full((1, 128), marks[j], jnp.float32)
        return carry

    lax.fori_loop(0, blocks // 8, place, 0)


def pack(home, tile, forces, offsets, bx, by, bz, devices):
    smem = pl.BlockSpec(memory_space=pltpu.SMEM)
    vmem = pl.BlockSpec(memory_space=pltpu.VMEM)
    blocks = home.shape[0]
    return pl.pallas_call(
        pack_kernel,
        out_shape=(
            jax.ShapeDtypeStruct((devices * ROWS, 128), jnp.float32),
            jax.ShapeDtypeStruct((blocks,), jnp.int32),
        ),
        in_specs=[smem, smem, vmem, vmem, vmem, vmem, vmem],
        out_specs=(vmem, smem),
        scratch_shapes=[pltpu.SMEM((devices,), jnp.int32)],
        name="pack",
    )(home, tile, forces, offsets, bx, by, bz)


def list_slots(tile_ref, list_ref, count):
    def step(s, n):
        list_ref[n] = s
        return n + (tile_ref[s] >= 0).astype(jnp.int32)

    total = lax.fori_loop(0, count, step, 0, unroll=8)

    @pl.when(total % 2 == 1)
    def _():
        list_ref[total] = list_ref[total - 1]

    return total


def slot_weights(recv_ref, slot):
    device, rank = slot // 2, slot % 2
    row0 = pl.multiple_of(device * ROWS + 24 * rank, 8)
    off = recv_ref[pl.ds(row0, 8), :]
    base = recv_ref[pl.ds(row0 + 8, 8), :]
    square = 1.0 + 4.0 * off - 4.0 * off * off
    rad = square * lax.rsqrt(square)
    low, high = 3.0 - 2.0 * off, 1.0 + 2.0 * off
    weights = [(low - rad) * 0.125, (low + rad) * 0.125, (high + rad) * 0.125, (high - rad) * 0.125]
    corners = [base, base + 1.0, base + 2.0, base + 3.0]
    return corners, weights


def spread_rows(cell, corners, weights, dtype):
    shape = cell.shape
    out = jnp.zeros(shape, dtype)
    for corner, weight in zip(corners, weights):
        out = jnp.where(cell == corner, weight, out)
    return out


def rows_of(values, row, sublanes, dtype):
    return [jnp.broadcast_to(v[row : row + 1, :], (sublanes, 128)).astype(dtype) for v in values]


def weights_x(corners, weights, q):
    cs, ws = rows_of(corners, q * 3, 8, jnp.float32), rows_of(weights, q * 3, 8, jnp.float32)
    cell = lax.broadcasted_iota(jnp.int32, (8, 128), 0).astype(jnp.float32)
    return [spread_rows(cell + 8.0 * k, cs, ws, jnp.float32) for k in range(TX // 8)]


def weights_y(corners, weights, q):
    cs, ws = rows_of(corners, q * 3 + 1, 8, jnp.float32), rows_of(weights, q * 3 + 1, 8, jnp.float32)
    cell = lax.broadcasted_iota(jnp.int32, (8, 128), 0).astype(jnp.float32)
    return spread_rows(cell, cs, ws, jnp.float32)


def weights_z(corners, weights, q, depth):
    cs, ws = rows_of(corners, q * 3 + 2, 16, jnp.bfloat16), rows_of(weights, q * 3 + 2, 16, jnp.bfloat16)
    cell = lax.broadcasted_iota(jnp.int32, (16, 128), 0).astype(jnp.float32)
    return [spread_rows((cell + 16.0 * k).astype(jnp.bfloat16), cs, ws, jnp.bfloat16) for k in range(depth // 16)]


def spread_kernel(tile_ref, recv_ref, velocity_ref, forced_ref, list_ref, acc_ref):
    depth = velocity_ref.shape[3]
    tiles_y = velocity_ref.shape[2] // TY
    slots = tile_ref.shape[0]
    total = list_slots(tile_ref, list_ref, slots)
    acc_ref[...] = jnp.zeros(acc_ref.shape, jnp.float32)

    def piece(slot):
        corners, weights = slot_weights(recv_ref, slot)
        device, rank = slot // 2, slot % 2
        kernel_xy, weighted = [], []
        for q in range(2):
            wx = weights_x(corners, weights, q)
            wy = weights_y(corners, weights, q)
            columns = [
                jnp.broadcast_to(wx[i // 8][i % 8 : i % 8 + 1, :], (8, 128)) * wy for i in range(TX)
            ]
            kernel_xy.append(jnp.concatenate(columns, axis=0).astype(jnp.bfloat16))
            wz = weights_z(corners, weights, q, depth)
            parts = []
            for c in range(3):
                row = device * ROWS + force_row(rank, q * 3 + c)
                force = jnp.broadcast_to(recv_ref[pl.ds(row, 1), :], (16, 128)).astype(jnp.bfloat16)
                parts += [w * force for w in wz]
            weighted.append(jnp.concatenate(parts, axis=0))
        a = jnp.concatenate(kernel_xy, axis=1)
        b = jnp.concatenate(weighted, axis=1)
        return lax.dot_general(a, b, (((1,), (1,)), ((), ())), preferred_element_type=jnp.float32)

    def add(tile, out):
        x0 = (tile // tiles_y) * TX
        y0 = pl.multiple_of((tile % tiles_y) * TY, TY)
        for c in range(3):
            block = out[:, c * depth : (c + 1) * depth].reshape(TX, TY, depth)
            here = (c, pl.ds(x0, TX), pl.ds(y0, TY), slice(None))
            acc_ref[here] = acc_ref[here] + block

    def pair(n, carry):
        first, second = list_ref[2 * n], list_ref[2 * n + 1]
        out0, out1 = piece(first), piece(second)
        add(tile_ref[first], out0)

        @pl.when(2 * n + 1 < total)
        def _():
            add(tile_ref[second], out1)

        return carry

    lax.fori_loop(0, (total + 1) // 2, pair, 0)
    forced_ref[...] = velocity_ref[...] + time_step * acc_ref[...]


def spread(tile, recv, velocity):
    smem = pl.BlockSpec(memory_space=pltpu.SMEM)
    vmem = pl.BlockSpec(memory_space=pltpu.VMEM)
    return pl.pallas_call(
        spread_kernel,
        out_shape=jax.ShapeDtypeStruct(velocity.shape, jnp.float32),
        in_specs=[smem, vmem, vmem],
        out_specs=vmem,
        scratch_shapes=[
            pltpu.SMEM((tile.shape[0] + 8,), jnp.int32),
            pltpu.VMEM(velocity.shape, jnp.float32),
        ],
        compiler_params=pltpu.CompilerParams(vmem_limit_bytes=40 << 20),
        name="spread",
    )(tile, recv, velocity)


def sweep_kernel(tile_ref, recv_ref, forced_ref, xlo_ref, xhi_ref, ylo_ref, yhi_ref, next_ref, reply_ref, list_ref, pad_ref, tiled_ref):
    _, size_x, size_y, depth = forced_ref.shape
    tiles_y = size_y // TY
    slots = tile_ref.shape[0]
    total = list_slots(tile_ref, list_ref, slots)
    pad_ref[:, 1 : size_x + 1, 8 : size_y + 8, :] = forced_ref[...]
    pad_ref[:, 0, 8 : size_y + 8, :] = xlo_ref[...]
    pad_ref[:, size_x + 1, 8 : size_y + 8, :] = xhi_ref[...]
    pad_ref[:, 1 : size_x + 1, 7, :] = ylo_ref[...]
    pad_ref[:, 1 : size_x + 1, size_y + 8, :] = yhi_ref[...]
    lane = lax.broadcasted_iota(jnp.int32, (TY, depth), 1)
    first_lane, last_lane = lane == 0, lane == depth - 1

    def column(x2, carry):
        for ty in range(tiles_y):
            y0 = 8 + ty * TY
            halves = [[], [], []]
            for dx in range(2):
                x = x2 * 2 + dx + 1
                centre = [pad_ref[c, x, y0 : y0 + TY, :] for c in range(3)]
                for c in range(3):
                    plus_x = pad_ref[c, x + 1, y0 : y0 + TY, :]
                    minus_x = pad_ref[c, x - 1, y0 : y0 + TY, :]
                    plus_y = pad_ref[c, x, y0 + 1 : y0 + TY + 1, :]
                    minus_y = pad_ref[c, x, y0 - 1 : y0 + TY - 1, :]
                    plus_z = jnp.where(last_lane, 0.0, pltpu.roll(centre[c], depth - 1, 1))
                    minus_z = jnp.where(first_lane, 0.0, pltpu.roll(centre[c], 1, 1))
                    laplace = plus_x + minus_x + plus_y + minus_y + plus_z + minus_z - 6.0 * centre[c]
                    advect = (
                        centre[0] * (plus_x - minus_x)
                        + centre[1] * (plus_y - minus_y)
                        + centre[2] * (plus_z - minus_z)
                    ) * 0.5
                    value = centre[c] + time_step * (viscosity * laplace - advect)
                    next_ref[c, x - 1, ty * TY : (ty + 1) * TY, :] = value
                    halves[c].append(value)
            tile = (x2 // (TX // 2)) * tiles_y + ty
            for c in range(3):
                row = pl.multiple_of((tile * 3 + c) * (TX * TY) + (x2 % (TX // 2)) * 16, 16)
                tiled_ref[pl.ds(row, 16), :] = jnp.concatenate(halves[c], axis=0).astype(jnp.bfloat16)
        return carry

    lax.fori_loop(0, size_x // 2, column, 0)

    def fetch(slot):
        corners, weights = slot_weights(recv_ref, slot)
        tile = tile_ref[slot]
        wz = jnp.concatenate(
            [jnp.concatenate(weights_z(corners, weights, q, depth), axis=0) for q in range(2)], axis=1
        )
        row = pl.multiple_of(tile * (3 * TX * TY), 16)
        field = tiled_ref[pl.ds(row, 3 * TX * TY), :]
        return corners, weights, lax.dot_general(
            field, wz, (((1,), (0,)), ((), ())), preferred_element_type=jnp.float32
        )

    def finish(slot, corners, weights, along):
        for q in range(2):
            wx = weights_x(corners, weights, q)
            wy = weights_y(corners, weights, q)
            wide = [jnp.broadcast_to(wx[i // 8][i % 8 : i % 8 + 1, :], (8, 128)) for i in range(TX)]
            for c in range(3):
                total_c = None
                for i in range(TX):
                    row = c * TX * TY + i * TY
                    term = wide[i] * along[row : row + TY, q * 128 : (q + 1) * 128]
                    total_c = term if total_c is None else total_c + term
                result = jnp.sum(total_c * wy, axis=0, keepdims=True)
                reply_ref[pl.ds(slot * 8 + q * 3 + c, 1), :] = result

    def pair(n, carry):
        first, second = list_ref[2 * n], list_ref[2 * n + 1]
        got0, got1 = fetch(first), fetch(second)
        finish(first, *got0)
        finish(second, *got1)
        return carry

    lax.fori_loop(0, (total + 1) // 2, pair, 0)


def sweep(tile, recv, forced, xlo, xhi, ylo, yhi):
    smem = pl.BlockSpec(memory_space=pltpu.SMEM)
    vmem = pl.BlockSpec(memory_space=pltpu.VMEM)
    _, size_x, size_y, depth = forced.shape
    slots = tile.shape[0]
    return pl.pallas_call(
        sweep_kernel,
        out_shape=(
            jax.ShapeDtypeStruct(forced.shape, jnp.float32),
            jax.ShapeDtypeStruct((slots * 8, 128), jnp.float32),
        ),
        in_specs=[smem] + [vmem] * 6,
        out_specs=(vmem, vmem),
        scratch_shapes=[
            pltpu.SMEM((slots + 8,), jnp.int32),
            pltpu.VMEM((3, size_x + 2, size_y + 16, depth), jnp.float32),
            pltpu.VMEM((3 * size_x * size_y, depth), jnp.bfloat16),
        ],
        compiler_params=pltpu.CompilerParams(vmem_limit_bytes=40 << 20),
        name="sweep",
    )(tile, recv, forced, xlo, xhi, ylo, yhi)


def gather_kernel(slot_ref, back_ref, out_ref):
    blocks = out_ref.shape[1]

    def take(group, carry):
        b0 = pl.multiple_of(group * 8, 8)
        starts = [slot_ref[b0 + j] * 8 for j in range(8)]
        for q in range(2):
            for c in range(3):
                rows = [back_ref[pl.ds(start + q * 3 + c, 1), :] for start in starts]
                out_ref[c, pl.ds(b0, 8), q * 128 : (q + 1) * 128] = jnp.concatenate(rows, axis=0)
        return carry

    lax.fori_loop(0, blocks // 8, take, 0)


def gather(slot, back):
    smem = pl.BlockSpec(memory_space=pltpu.SMEM)
    vmem = pl.BlockSpec(memory_space=pltpu.VMEM)
    return pl.pallas_call(
        gather_kernel,
        out_shape=jax.ShapeDtypeStruct((3, slot.shape[0], 256), jnp.float32),
        in_specs=[smem, vmem],
        out_specs=vmem,
        name="gather",
    )(slot, back)


def neighbour(value, axis, step):
    count = lax.axis_size(axis)
    return lax.ppermute(value, axis, [(i, i + step) for i in range(count) if 0 <= i + step < count])


def exchange(rows, devices):
    shaped = rows.reshape(devices, rows.shape[0] // devices, 128)
    return lax.all_to_all(shaped, AXES, split_axis=0, concat_axis=0, tiled=True)


def body(velocity, forces, offsets, base_x, base_y, base_z, home_device, home_tile):
    devices = lax.axis_size("gx") * lax.axis_size("gy")
    send, slot = pack(
        home_device[:, 0],
        home_tile,
        jnp.transpose(forces, (1, 0, 2)),
        jnp.transpose(offsets, (1, 0, 2)),
        base_x,
        base_y,
        base_z,
        devices,
    )
    recv = exchange(send, devices)
    tile = recv[:, 14:16, 0].astype(jnp.int32).reshape(-1)
    recv = recv.reshape(devices * ROWS, 128)
    forced = spread(tile, recv, velocity)
    xlo = neighbour(forced[:, -1], "gx", 1)
    xhi = neighbour(forced[:, 0], "gx", -1)
    ylo = neighbour(forced[:, :, -1], "gy", 1)
    yhi = neighbour(forced[:, :, 0], "gy", -1)
    velocity_next, reply = sweep(tile, recv, forced, xlo, xhi, ylo, yhi)
    back = exchange(reply, devices).reshape(-1, 128)
    fibre = gather(slot, back)
    return velocity_next, jnp.transpose(fibre, (1, 0, 2))


def solution(mesh):
    return jax.shard_map(
        body,
        mesh=mesh,
        in_specs=(
            P(None, "gx", "gy", None),
            P(AXES, None, None),
            P(AXES, None, None),
            P(AXES, None),
            P(AXES, None),
            P(AXES, None),
            P(AXES, None),
            P(AXES),
        ),
        out_specs=(P(None, "gx", "gy", None), P(AXES, None, None)),
        check_vma=False,
    )
```

```python
import jax
import jax.numpy as jnp
from jax import lax
from jax.experimental import pallas as pl
from jax.experimental.pallas import tpu as pltpu
from jax.sharding import PartitionSpec as P

TX = 16
TY = 8
ROWS = 40
WROWS = 40
UNROLL = 8
LIST_SPARE = UNROLL + 8
AXES = ("gx", "gy")

time_step = 0.4
viscosity = 0.15


def force_row(rank, idx):
    k, odd = idx // 2, idx % 2
    return jnp.where(rank == 0, 16 + idx, (6, 30, 38)[k] + odd)


def pack_kernel(home_ref, tile_ref, forces_ref, offsets_ref, bx_ref, by_ref, bz_ref, send_ref, slot_ref, count_ref):
    blocks = forces_ref.shape[1]
    devices = send_ref.shape[0] // ROWS

    def clear(d, carry):
        count_ref[d] = 0
        send_ref[pl.ds(d * ROWS + 14, 2), :] = jnp.full((2, 128), -1.0, jnp.float32)
        return carry

    lax.fori_loop(0, devices, clear, 0, unroll=8)

    def place(group, carry):
        b0 = pl.multiple_of(group * 8, 8)
        starts, marks = [], []
        for j in range(8):
            home = home_ref[b0 + j]
            rank = count_ref[home]
            count_ref[home] = rank + 1
            slot_ref[b0 + j] = home * 2 + rank
            row0 = home * ROWS
            pairs = [row0 + jnp.where(rank == 0, 16 + 2 * k, (6, 30, 38)[k]) for k in range(3)]
            starts.append((pl.multiple_of(row0 + 24 * rank, 8), pairs))
            marks.append((row0 + 14 + rank, tile_ref[b0 + j].astype(jnp.float32)))
        for q in range(2):
            lanes = slice(q * 128, (q + 1) * 128)
            for v in range(3):
                idx = q * 3 + v
                off = offsets_ref[v, pl.ds(b0, 8), lanes]
                base = (bx_ref, by_ref, bz_ref)[v][pl.ds(b0, 8), lanes].astype(jnp.float32)
                force = forces_ref[v, pl.ds(b0, 8), lanes]
                for j, (start, pairs) in enumerate(starts):
                    send_ref[pl.ds(start + idx, 1), :] = off[j : j + 1, :]
                    send_ref[pl.ds(start + 8 + idx, 1), :] = base[j : j + 1, :]
                    send_ref[pl.ds(pairs[idx // 2] + idx % 2, 1), :] = force[j : j + 1, :]
        for row, mark in marks:
            send_ref[pl.ds(row, 1), :] = jnp.full((1, 128), mark, jnp.float32)
        return carry

    lax.fori_loop(0, blocks // 8, place, 0)


def pack(home, tile, forces, offsets, bx, by, bz, devices):
    smem = pl.BlockSpec(memory_space=pltpu.SMEM)
    vmem = pl.BlockSpec(memory_space=pltpu.VMEM)
    blocks = home.shape[0]
    return pl.pallas_call(
        pack_kernel,
        out_shape=(
            jax.ShapeDtypeStruct((devices * ROWS, 128), jnp.float32),
            jax.ShapeDtypeStruct((blocks,), jnp.int32),
        ),
        in_specs=[smem, smem, vmem, vmem, vmem, vmem, vmem],
        out_specs=(vmem, smem),
        scratch_shapes=[pltpu.SMEM((devices,), jnp.int32)],
        name="pack",
    )(home, tile, forces, offsets, bx, by, bz)


def read_tiles(recv_ref, tile_vmem, tile_smem, sem):
    devices = recv_ref.shape[0] // ROWS
    lane = lax.broadcasted_iota(jnp.int32, (2, 128), 1)
    for first in range(0, devices, 128):
        found = jnp.full((2, 128), -1.0, jnp.float32)
        for d in range(first, min(first + 128, devices)):
            found = jnp.where(lane == d - first, recv_ref[d * ROWS + 14 : d * ROWS + 16, :], found)
        tile_vmem[first // 64 : first // 64 + 2, :] = found.astype(jnp.int32)
    copy = pltpu.make_async_copy(tile_vmem, tile_smem, sem)
    copy.start()
    copy.wait()


def list_slots(tile_smem, list_ref, mark_ref, devices, spare):
    def step(d, n):
        for rank in range(2):
            tile = tile_smem[(d // 128) * 2 + rank, d % 128]
            list_ref[n] = d * 2 + rank
            mark_ref[n] = tile
            n = n + (tile >= 0).astype(jnp.int32)
        return n

    end = lax.fori_loop(0, devices, step, 0, unroll=4)
    for extra in range(UNROLL - 1):
        list_ref[end + extra] = list_ref[jnp.maximum(end - 1, 0)]
        mark_ref[end + extra] = spare
    steps = (end + UNROLL - 1) // UNROLL
    list_ref[list_ref.shape[0] - 1] = steps
    return steps, end


def weigh_slots(recv_ref, weight_ref, slots):
    row = lax.broadcasted_iota(jnp.int32, (8, 128), 0)
    along_z = (row == 2) | (row == 5)

    def one(slot):
        start = pl.multiple_of(lax.shift_right_logical(slot, 1) * ROWS + 24 * (slot & 1), 8)
        off = recv_ref[pl.ds(start, 8), :]
        base = recv_ref[pl.ds(start + 8, 8), :]
        square = 1.0 + 4.0 * off - 4.0 * off * off
        rad = square * lax.rsqrt(square)
        low, high = 3.0 - 2.0 * off, 1.0 + 2.0 * off
        block = jnp.floor(base * 0.0625)
        to = pl.multiple_of(slot * WROWS, 8)
        weight_ref[pl.ds(to, 8), :] = jnp.where(along_z, base - 16.0 * block, base)
        weight_ref[pl.ds(to + 6, 1), :] = block[2:3, :]
        weight_ref[pl.ds(to + 7, 1), :] = block[5:6, :]
        weight_ref[pl.ds(to + 8, 8), :] = (low - rad) * 0.125
        weight_ref[pl.ds(to + 16, 8), :] = (low + rad) * 0.125
        weight_ref[pl.ds(to + 24, 8), :] = (high + rad) * 0.125
        weight_ref[pl.ds(to + 32, 8), :] = (high - rad) * 0.125

    def four(n, carry):
        for k in range(4):
            one(n * 4 + k)
        return carry

    lax.fori_loop(0, slots // 4, four, 0)


def wide(ref, row, dtype=jnp.float32):
    value = ref[pl.ds(row, 8, stride=0), :]
    if dtype == jnp.float32:
        return value
    return jnp.concatenate([value, value], axis=0).astype(dtype)


def picked(base, weights, cells):
    out = jnp.zeros(base.shape, base.dtype)
    for weight, cell in zip(weights, cells):
        out = jnp.where(base == cell, weight, out)
    return out


def cells_from(first, sublanes, dtype):
    cell = lax.broadcasted_iota(jnp.int32, (sublanes, 128), 0) + first
    return cell.astype(jnp.float32).astype(dtype)


def cell_table():
    f32, half = jnp.float32, jnp.bfloat16
    table = {(n, f32): cells_from(n, 8, f32) for n in range(-3, 9)}
    table.update({(n, half): cells_from(n, 16, half) for n in (-3, -2, -1, 0, 13, 14, 15)})
    return table


def weights_x(weight_ref, to, q, table):
    base = wide(weight_ref, to + q * 3)
    ws = [wide(weight_ref, to + 8 + 8 * m + q * 3) for m in range(4)]
    return [picked(base, ws, [table[8 * k - m, jnp.float32] for m in range(4)]) for k in range(TX // 8)]


def weights_y(weight_ref, to, q, table):
    base = wide(weight_ref, to + q * 3 + 1)
    ws = [wide(weight_ref, to + 8 + 8 * m + q * 3 + 1) for m in range(4)]
    return picked(base, ws, [table[-m, jnp.float32] for m in range(4)])


def weights_z(weight_ref, to, q, depth, table):
    half = jnp.bfloat16
    base = wide(weight_ref, to + q * 3 + 2, half)
    block = wide(weight_ref, to + 6 + q, half)
    ws = [wide(weight_ref, to + 8 + 8 * m + q * 3 + 2, half) for m in range(4)]
    low = picked(base, ws, [table[-m, half] for m in range(4)])
    high = picked(base, ws[1:], [table[16 - m, half] for m in range(1, 4)])
    zero = jnp.zeros((16, 128), half)
    here = [block == jnp.full((16, 128), k, half) for k in range(depth // 16)]
    out = []
    for k in range(depth // 16):
        before = jnp.where(here[k - 1], high, zero) if k else zero
        out.append(jnp.where(here[k], low, before))
    return out


def spread_kernel(
    recv_ref, velocity_hbm, forced_ref, weight_ref, xlo_ref, xhi_ref, ylo_ref, yhi_ref, list_ref, mark_ref,
    velocity_ref, acc_ref, wide_ref, tile_vmem, tile_smem, sems,
):
    fetch = pltpu.make_async_copy(velocity_hbm, velocity_ref, sems.at[0])
    fetch.start()
    depth = velocity_ref.shape[3]
    size_x, size_y = velocity_ref.shape[1:3]
    tiles_y = size_y // TY
    tiles = (size_x // TX) * tiles_y
    slots = 2 * (recv_ref.shape[0] // ROWS)
    read_tiles(recv_ref, tile_vmem, tile_smem, sems.at[1])
    steps, end = list_slots(tile_smem, list_ref, mark_ref, slots // 2, tiles)
    weigh_slots(recv_ref, weight_ref, slots)
    tile_rows = 3 * TX * TY

    def clear(n, carry):
        acc_ref[pl.ds(pl.multiple_of(n * tile_rows, 8), tile_rows), :] = jnp.zeros((tile_rows, depth), jnp.float32)
        return carry

    lax.fori_loop(0, tiles, clear, 0)

    table = cell_table()

    def build(slot, k):
        device, rank = lax.shift_right_logical(slot, 1), slot & 1
        to = pl.multiple_of(slot * WROWS, 8)
        kernel_xy, weighted = [], []
        for q in range(2):
            wx = weights_x(weight_ref, to, q, table)
            at = (2 * k + q) * TX
            for part in range(TX // 8):
                wide_ref[at + part * 8 : at + part * 8 + 8, :] = wx[part]
            wy = weights_y(weight_ref, to, q, table)
            columns = [wide(wide_ref, at + i) * wy for i in range(TX)]
            kernel_xy.append(jnp.concatenate(columns, axis=0).astype(jnp.bfloat16))
            wz = weights_z(weight_ref, to, q, depth, table)
            parts = []
            for c in range(3):
                force = wide(recv_ref, device * ROWS + force_row(rank, q * 3 + c), jnp.bfloat16)
                parts += [w * force for w in wz]
            weighted.append(jnp.concatenate(parts, axis=0))
        return lax.dot_general(
            jnp.concatenate(kernel_xy, axis=1),
            jnp.concatenate(weighted, axis=1),
            (((1,), (1,)), ((), ())),
            preferred_element_type=jnp.float32,
        )

    def add(mark, out):
        for c in range(3):
            here = pl.ds(pl.multiple_of(mark * tile_rows + c * TX * TY, 8), TX * TY)
            acc_ref[here, :] = acc_ref[here, :] + out[:, c * depth : (c + 1) * depth]

    def step(n, carry):
        outs = [build(list_ref[UNROLL * n + k], k) for k in range(UNROLL)]
        for k in range(UNROLL):
            add(mark_ref[UNROLL * n + k], outs[k])
        return carry

    lax.fori_loop(0, steps, step, 0)
    for extra in range(UNROLL - 1):
        mark_ref[end + extra] = mark_ref[jnp.maximum(end - 1, 0)]
    fetch.wait()

    def finish(x, carry):
        for c in range(3):
            for ty in range(tiles_y):
                row = ((x // TX) * tiles_y + ty) * tile_rows + c * TX * TY + (x % TX) * TY
                here = (c, x, slice(ty * TY, (ty + 1) * TY), slice(None))
                value = velocity_ref[here] + time_step * acc_ref[pl.ds(pl.multiple_of(row, 8), TY), :]
                forced_ref[here] = value
                if ty == 0:
                    ylo_ref[c, pl.ds(x, 1), :] = value[0:1, :]
                if ty == tiles_y - 1:
                    yhi_ref[c, pl.ds(x, 1), :] = value[TY - 1 : TY, :]
        return carry

    lax.fori_loop(0, size_x, finish, 0)
    xlo_ref[...] = forced_ref[:, 0]
    xhi_ref[...] = forced_ref[:, size_x - 1]


def spread(recv, velocity):
    smem = pl.BlockSpec(memory_space=pltpu.SMEM)
    vmem = pl.BlockSpec(memory_space=pltpu.VMEM)
    hbm = pl.BlockSpec(memory_space=pl.ANY)
    _, size_x, size_y, depth = velocity.shape
    devices = recv.shape[0] // ROWS
    slots = 2 * devices
    tiles = (size_x // TX) * (size_y // TY)
    tile_shape = (2 * pl.cdiv(devices, 128), 128)
    x_face = jax.ShapeDtypeStruct((3, size_y, depth), jnp.float32)
    y_face = jax.ShapeDtypeStruct((3, size_x, depth), jnp.float32)
    table = jax.ShapeDtypeStruct((slots + LIST_SPARE,), jnp.int32)
    return pl.pallas_call(
        spread_kernel,
        out_shape=(
            jax.ShapeDtypeStruct(velocity.shape, jnp.float32),
            jax.ShapeDtypeStruct((slots * WROWS, 128), jnp.float32),
            x_face,
            x_face,
            y_face,
            y_face,
            table,
            table,
        ),
        in_specs=[vmem, hbm],
        out_specs=(vmem,) * 6 + (smem, smem),
        scratch_shapes=[
            pltpu.VMEM(velocity.shape, jnp.float32),
            pltpu.VMEM(((tiles + 1) * 3 * TX * TY, depth), jnp.float32),
            pltpu.VMEM((2 * UNROLL * TX, 128), jnp.float32),
            pltpu.VMEM(tile_shape, jnp.int32),
            pltpu.SMEM(tile_shape, jnp.int32),
            pltpu.SemaphoreType.DMA((2,)),
        ],
        compiler_params=pltpu.CompilerParams(
            vmem_limit_bytes=24 << 20
        ),
        name="spread",
    )(recv, velocity)


def sweep_kernel(
    list_ref, mark_ref, weight_ref, forced_ref, xlo_ref, xhi_ref, ylo_ref, yhi_ref, next_hbm, reply_ref,
    next_ref, pad_ref, tiled_ref, wide_ref, sem,
):
    _, size_x, size_y, depth = forced_ref.shape
    tiles_y = size_y // TY
    tiles = (size_x // TX) * tiles_y
    steps = list_ref[list_ref.shape[0] - 1]
    pad_ref[:, 1 : size_x + 1, 8 : size_y + 8, :] = forced_ref[...]
    pad_ref[:, 0, 8 : size_y + 8, :] = xlo_ref[...]
    pad_ref[:, size_x + 1, 8 : size_y + 8, :] = xhi_ref[...]
    pad_ref[:, 1 : size_x + 1, 7, :] = ylo_ref[...]
    pad_ref[:, 1 : size_x + 1, size_y + 8, :] = yhi_ref[...]
    lane = lax.broadcasted_iota(jnp.int32, (TY, depth), 1)
    first_lane, last_lane = lane == 0, lane == depth - 1

    def column(x2, carry):
        for ty in range(tiles_y):
            y0 = 8 + ty * TY
            halves = [[], [], []]
            for dx in range(2):
                x = x2 * 2 + dx + 1
                centre = [pad_ref[c, x, y0 : y0 + TY, :] for c in range(3)]
                for c in range(3):
                    plus_x = pad_ref[c, x + 1, y0 : y0 + TY, :]
                    minus_x = pad_ref[c, x - 1, y0 : y0 + TY, :]
                    plus_y = pad_ref[c, x, y0 + 1 : y0 + TY + 1, :]
                    minus_y = pad_ref[c, x, y0 - 1 : y0 + TY - 1, :]
                    plus_z = jnp.where(last_lane, 0.0, pltpu.roll(centre[c], depth - 1, 1))
                    minus_z = jnp.where(first_lane, 0.0, pltpu.roll(centre[c], 1, 1))
                    laplace = plus_x + minus_x + plus_y + minus_y + plus_z + minus_z - 6.0 * centre[c]
                    advect = (
                        centre[0] * (plus_x - minus_x)
                        + centre[1] * (plus_y - minus_y)
                        + centre[2] * (plus_z - minus_z)
                    ) * 0.5
                    value = centre[c] + time_step * (viscosity * laplace - advect)
                    next_ref[c, x - 1, ty * TY : (ty + 1) * TY, :] = value
                    halves[c].append(value)
            tile = (x2 // (TX // 2)) * tiles_y + ty
            for c in range(3):
                row = pl.multiple_of((tile * 3 + c) * (TX * TY) + (x2 % (TX // 2)) * 16, 16)
                tiled_ref[pl.ds(row, 16), :] = jnp.concatenate(halves[c], axis=0).astype(jnp.bfloat16)
        return carry

    lax.fori_loop(0, size_x // 2, column, 0)
    store = pltpu.make_async_copy(next_ref, next_hbm, sem)
    store.start()

    table = cell_table()

    def build(slot, mark, k):
        to = pl.multiple_of(slot * WROWS, 8)
        along_z = []
        for q in range(2):
            wx = weights_x(weight_ref, to, q, table)
            at = (2 * k + q) * TX
            for part in range(TX // 8):
                wide_ref[at + part * 8 : at + part * 8 + 8, :] = wx[part]
            along_z.append(jnp.concatenate(weights_z(weight_ref, to, q, depth, table), axis=0))
        row = pl.multiple_of(mark * (3 * TX * TY), 16)
        return lax.dot_general(
            tiled_ref[pl.ds(row, 3 * TX * TY), :],
            jnp.concatenate(along_z, axis=1),
            (((1,), (0,)), ((), ())),
            preferred_element_type=jnp.float32,
        )

    def finish(slot, along, k):
        to = pl.multiple_of(slot * WROWS, 8)
        for q in range(2):
            at = (2 * k + q) * TX
            sums = [None] * 3
            for i in range(TX):
                weight = wide(wide_ref, at + i)
                for c in range(3):
                    row = c * TX * TY + i * TY
                    term = weight * along[row : row + TY, q * 128 : (q + 1) * 128]
                    sums[c] = term if sums[c] is None else sums[c] + term
            wy = weights_y(weight_ref, to, q, table)
            for c in range(3):
                result = jnp.sum(sums[c] * wy, axis=0, keepdims=True)
                reply_ref[pl.ds(slot * 8 + q * 3 + c, 1), :] = result

    def step(n, carry):
        outs = [build(list_ref[UNROLL * n + k], mark_ref[UNROLL * n + k], k) for k in range(UNROLL)]
        for k in range(UNROLL):
            finish(list_ref[UNROLL * n + k], outs[k], k)
        return carry

    lax.fori_loop(0, steps, step, 0)
    store.wait()


def sweep(slot_list, marks, weights, forced, xlo, xhi, ylo, yhi):
    smem = pl.BlockSpec(memory_space=pltpu.SMEM)
    vmem = pl.BlockSpec(memory_space=pltpu.VMEM)
    hbm = pl.BlockSpec(memory_space=pl.ANY)
    _, size_x, size_y, depth = forced.shape
    slots = weights.shape[0] // WROWS
    return pl.pallas_call(
        sweep_kernel,
        out_shape=(
            jax.ShapeDtypeStruct(forced.shape, jnp.float32),
            jax.ShapeDtypeStruct((slots * 8, 128), jnp.float32),
        ),
        in_specs=[smem] * 2 + [vmem] * 6,
        out_specs=(hbm, vmem),
        scratch_shapes=[
            pltpu.VMEM(forced.shape, jnp.float32),
            pltpu.VMEM((3, size_x + 2, size_y + 16, depth), jnp.float32),
            pltpu.VMEM((3 * size_x * size_y, depth), jnp.bfloat16),
            pltpu.VMEM((2 * UNROLL * TX, 128), jnp.float32),
            pltpu.SemaphoreType.DMA,
        ],
        compiler_params=pltpu.CompilerParams(vmem_limit_bytes=24 << 20),
        name="sweep",
    )(slot_list, marks, weights, forced, xlo, xhi, ylo, yhi)


def gather_kernel(slot_ref, back_ref, out_ref):
    blocks = out_ref.shape[1]

    def take(group, carry):
        b0 = pl.multiple_of(group * 8, 8)
        starts = [slot_ref[b0 + j] * 8 for j in range(8)]
        for q in range(2):
            for c in range(3):
                rows = [back_ref[pl.ds(start + q * 3 + c, 1), :] for start in starts]
                out_ref[c, pl.ds(b0, 8), q * 128 : (q + 1) * 128] = jnp.concatenate(rows, axis=0)
        return carry

    lax.fori_loop(0, blocks // 8, take, 0)


def gather(slot, back):
    smem = pl.BlockSpec(memory_space=pltpu.SMEM)
    vmem = pl.BlockSpec(memory_space=pltpu.VMEM)
    return pl.pallas_call(
        gather_kernel,
        out_shape=jax.ShapeDtypeStruct((3, slot.shape[0], 256), jnp.float32),
        in_specs=[smem, vmem],
        out_specs=vmem,
        name="gather",
    )(slot, back)


def neighbour(value, axis, step):
    count = lax.axis_size(axis)
    return lax.ppermute(value, axis, [(i, i + step) for i in range(count) if 0 <= i + step < count])


def exchange(rows, devices):
    shaped = rows.reshape(devices, rows.shape[0] // devices, 128)
    return lax.all_to_all(shaped, AXES, split_axis=0, concat_axis=0, tiled=True)


def body(velocity, forces, offsets, base_x, base_y, base_z, home_device, home_tile):
    devices = lax.axis_size("gx") * lax.axis_size("gy")
    send, slot = pack(
        home_device[:, 0],
        home_tile,
        jnp.transpose(forces, (1, 0, 2)),
        jnp.transpose(offsets, (1, 0, 2)),
        base_x,
        base_y,
        base_z,
        devices,
    )
    recv = exchange(send, devices).reshape(devices * ROWS, 128)
    forced, weights, x_first, x_last, y_first, y_last, slot_list, marks = spread(recv, velocity)
    xlo = neighbour(x_last, "gx", 1)
    xhi = neighbour(x_first, "gx", -1)
    ylo = neighbour(y_last, "gy", 1)
    yhi = neighbour(y_first, "gy", -1)
    velocity_next, reply = sweep(slot_list, marks, weights, forced, xlo, xhi, ylo, yhi)
    back = exchange(reply, devices).reshape(-1, 128)
    fibre = gather(slot, back)
    return velocity_next, jnp.transpose(fibre, (1, 0, 2))


def solution(mesh):
    return jax.shard_map(
        body,
        mesh=mesh,
        in_specs=(
            P(None, "gx", "gy", None),
            P(AXES, None, None),
            P(AXES, None, None),
            P(AXES, None),
            P(AXES, None),
            P(AXES, None),
            P(AXES, None),
            P(AXES),
        ),
        out_specs=(P(None, "gx", "gy", None), P(AXES, None, None)),
        check_vma=False,
    )
```

```python
import jax
import jax.numpy as jnp
from jax import lax
from jax.experimental import pallas as pl
from jax.experimental.pallas import tpu as pltpu
from jax.sharding import PartitionSpec as P

TX = 16
TY = 8
FIRST = 24
REST = 16
MARK_BITS = 5
MARKS = 1 << MARK_BITS
WROWS = 40
UNROLL = 16
LIST_SPARE = UNROLL + 8
AXES = ("gx", "gy")

SMEM = pl.BlockSpec(memory_space=pltpu.SMEM)
VMEM = pl.BlockSpec(memory_space=pltpu.VMEM)
HBM = pl.BlockSpec(memory_space=pltpu.HBM)

time_step = 0.4
viscosity = 0.15


def pack_kernel(home_ref, tile_ref, forces_ref, offsets_ref, bx_ref, by_ref, bz_ref, first_ref, rest_ref, slot_ref, count_ref):
    blocks = forces_ref.shape[1]
    devices = first_ref.shape[0] // FIRST

    def clear(d, carry):
        count_ref[d] = 0
        first_ref[pl.ds(d * FIRST + 14, 2), :] = jnp.full((2, 128), -1.0, jnp.float32)
        return carry

    lax.fori_loop(0, devices, clear, 0, unroll=8)

    def put(send_ref, start, rows, forces, values):
        offsets, bases, force = values
        for idx in range(6):
            send_ref[pl.ds(start + idx, 1), :] = offsets[idx]
            send_ref[pl.ds(start + 8 + idx, 1), :] = bases[idx]
        for idx in forces:
            send_ref[pl.ds(start + rows[idx], 1), :] = force[idx]

    def place(group, carry):
        b0 = pl.multiple_of(group * 8, 8)
        offsets, bases, forces = [], [], []
        for q in range(2):
            lanes = slice(q * 128, (q + 1) * 128)
            for v in range(3):
                offsets.append(offsets_ref[v, pl.ds(b0, 8), lanes])
                bases.append((bx_ref, by_ref, bz_ref)[v][pl.ds(b0, 8), lanes].astype(jnp.float32))
                forces.append(forces_ref[v, pl.ds(b0, 8), lanes])
        for j in range(8):
            home = home_ref[b0 + j]
            rank = count_ref[home]
            count_ref[home] = rank + 1
            slot_ref[b0 + j] = home * 2 + rank
            mark = jnp.full((1, 128), tile_ref[b0 + j].astype(jnp.float32), jnp.float32)
            first_ref[pl.ds(home * FIRST + 14 + rank, 1), :] = mark
            values = [[x[j : j + 1, :] for x in group] for group in (offsets, bases, forces)]

            @pl.when(rank == 0)
            def _():
                put(first_ref, home * FIRST, range(16, 22), range(6), values)

            @pl.when(rank != 0)
            def _():
                put(rest_ref, home * REST, (None, None, 6, 7, 14, 15), range(2, 6), values)
                for idx in range(2):
                    first_ref[pl.ds(home * FIRST + 6 + idx, 1), :] = values[2][idx]

        return carry

    lax.fori_loop(0, blocks // 8, place, 0)


def pack(home, tile, forces, offsets, bx, by, bz, devices):
    blocks = home.shape[0]
    return pl.pallas_call(
        pack_kernel,
        out_shape=(
            pltpu.VMEM((devices * FIRST, 128), jnp.float32),
            pltpu.VMEM((devices * REST, 128), jnp.float32),
            jax.ShapeDtypeStruct((blocks,), jnp.int32),
        ),
        in_specs=[SMEM, SMEM] + [VMEM] * 5,
        out_specs=(VMEM, VMEM, SMEM),
        scratch_shapes=[pltpu.SMEM((devices,), jnp.int32)],
        name="pack",
    )(home, tile, forces, offsets, bx, by, bz)


def read_tiles(first_ref, tile_vmem, tile_smem, sem):
    devices = first_ref.shape[0] // FIRST
    lane = lax.broadcasted_iota(jnp.int32, (2, devices), 1)
    rank = lax.broadcasted_iota(jnp.int32, (2, devices), 0)
    found = jnp.full((2, devices), -1.0, jnp.float32)
    for d in range(devices):
        found = jnp.where(lane == d, first_ref[d * FIRST + 14 : d * FIRST + 16, :], found)
    tile = found.astype(jnp.int32)
    tile_vmem[...] = jnp.where(tile < 0, -1, (rank * devices + lane) * MARKS + tile)
    copy = pltpu.make_async_copy(tile_vmem, tile_smem, sem)
    copy.start()
    copy.wait()


def list_slots(tile_smem, rank, list_ref, start):
    def step(d, n):
        code = tile_smem[rank, d]
        list_ref[n] = code
        return n + 1 + lax.shift_right_arithmetic(code, 31)

    return lax.fori_loop(0, tile_smem.shape[1], step, start, unroll=16)


def pad_list(list_ref, end, spare):
    last = list_ref[jnp.maximum(end - 1, 0)]
    for extra in range(UNROLL - 1):
        list_ref[end + extra] = last if spare is None else spare
    list_ref[list_ref.shape[0] - 1] = (end + UNROLL - 1) // UNROLL


def weigh_slots(recv_ref, stride, weight_ref, first, devices):
    row = lax.broadcasted_iota(jnp.int32, (8, 128), 0)
    along_z = (row == 2) | (row == 5)

    def one(device):
        start = pl.multiple_of(device * stride, 8)
        off = recv_ref[pl.ds(start, 8), :]
        base = recv_ref[pl.ds(start + 8, 8), :]
        square = 1.0 + 4.0 * off - 4.0 * off * off
        rad = square * lax.rsqrt(square)
        low, high = 3.0 - 2.0 * off, 1.0 + 2.0 * off
        block = jnp.floor(base * 0.0625)
        to = pl.multiple_of((first + device) * WROWS, 8)
        weight_ref[pl.ds(to, 8), :] = jnp.where(along_z, base - 16.0 * block, base)
        weight_ref[pl.ds(to + 6, 1), :] = block[2:3, :]
        weight_ref[pl.ds(to + 7, 1), :] = block[5:6, :]
        weight_ref[pl.ds(to + 8, 8), :] = (low - rad) * 0.125
        weight_ref[pl.ds(to + 16, 8), :] = (low + rad) * 0.125
        weight_ref[pl.ds(to + 24, 8), :] = (high + rad) * 0.125
        weight_ref[pl.ds(to + 32, 8), :] = (high - rad) * 0.125

    def four(n, carry):
        for k in range(4):
            one(n * 4 + k)
        return carry

    lax.fori_loop(0, devices // 4, four, 0)


def wide(ref, row, dtype=jnp.float32):
    value = ref[pl.ds(row, 8, stride=0), :]
    if dtype == jnp.float32:
        return value
    return jnp.concatenate([value, value], axis=0).astype(dtype)


def picked(base, weights, cells):
    out = jnp.zeros(base.shape, base.dtype)
    for weight, cell in zip(weights, cells):
        out = jnp.where(base == cell, weight, out)
    return out


def cells_from(first, sublanes, dtype):
    cell = lax.broadcasted_iota(jnp.int32, (sublanes, 128), 0) + first
    return cell.astype(jnp.float32).astype(dtype)


def cell_table():
    f32, half = jnp.float32, jnp.bfloat16
    table = {(n, f32): cells_from(n, 8, f32) for n in range(-3, 9)}
    table.update({(n, half): cells_from(n, 16, half) for n in (-3, -2, -1, 0, 13, 14, 15)})
    return table


def weights_x(weight_ref, to, q, table):
    base = wide(weight_ref, to + q * 3)
    ws = [wide(weight_ref, to + 8 + 8 * m + q * 3) for m in range(4)]
    return [picked(base, ws, [table[8 * k - m, jnp.float32] for m in range(4)]) for k in range(TX // 8)]


def weights_y(weight_ref, to, q, table):
    base = wide(weight_ref, to + q * 3 + 1)
    ws = [wide(weight_ref, to + 8 + 8 * m + q * 3 + 1) for m in range(4)]
    return picked(base, ws, [table[-m, jnp.float32] for m in range(4)])


def weights_z(weight_ref, to, q, depth, table):
    half = jnp.bfloat16
    base = wide(weight_ref, to + q * 3 + 2, half)
    block = wide(weight_ref, to + 6 + q, half)
    ws = [wide(weight_ref, to + 8 + 8 * m + q * 3 + 2, half) for m in range(4)]
    low = picked(base, ws, [table[-m, half] for m in range(4)])
    high = picked(base, ws[1:], [table[16 - m, half] for m in range(1, 4)])
    zero = jnp.zeros((16, 128), half)
    here = [block == jnp.full((16, 128), k, half) for k in range(depth // 16)]
    out = []
    for k in range(depth // 16):
        before = jnp.where(here[k - 1], high, zero) if k else zero
        out.append(jnp.where(here[k], low, before))
    return out


def spread_blocks(list_ref, weight_ref, force_rows, acc_ref, wide_ref, tiles, depth):
    tile_rows = 3 * TX * TY

    def clear(n, carry):
        acc_ref[pl.ds(pl.multiple_of(n * tile_rows, 8), tile_rows), :] = jnp.zeros((tile_rows, depth), jnp.float32)
        return carry

    lax.fori_loop(0, tiles, clear, 0)
    table = cell_table()

    def build(slot, k):
        to = pl.multiple_of(slot * WROWS, 8)
        kernel_xy, weighted = [], []
        for q in range(2):
            wx = weights_x(weight_ref, to, q, table)
            at = (2 * k + q) * TX
            for part in range(TX // 8):
                wide_ref[at + part * 8 : at + part * 8 + 8, :] = wx[part]
            wy = weights_y(weight_ref, to, q, table)
            columns = [wide(wide_ref, at + i) * wy for i in range(TX)]
            kernel_xy.append(jnp.concatenate(columns, axis=0).astype(jnp.bfloat16))
            wz = weights_z(weight_ref, to, q, depth, table)
            parts = []
            for c in range(3):
                force = wide(*force_rows(slot, q * 3 + c), jnp.bfloat16)
                parts += [w * force for w in wz]
            weighted.append(jnp.concatenate(parts, axis=0))
        return lax.dot_general(
            jnp.concatenate(kernel_xy, axis=1),
            jnp.concatenate(weighted, axis=1),
            (((1,), (1,)), ((), ())),
            preferred_element_type=jnp.float32,
        )

    def add(tile, out):
        for c in range(3):
            here = pl.ds(pl.multiple_of(tile * tile_rows + c * TX * TY, 8), TX * TY)
            acc_ref[here, :] = acc_ref[here, :] + out[:, c * depth : (c + 1) * depth]

    def step(n, carry):
        codes = [list_ref[UNROLL * n + k] for k in range(UNROLL)]
        outs = [build(lax.shift_right_logical(code, MARK_BITS), k) for k, code in enumerate(codes)]
        for code, out in zip(codes, outs):
            add(code & (MARKS - 1), out)
        return carry

    lax.fori_loop(0, list_ref[list_ref.shape[0] - 1], step, 0)


def spread_first_kernel(
    first_ref, acc_hbm, weight_hbm, rest_ref, all_ref,
    acc_ref, weight_ref, wide_ref, list_ref, tile_vmem, tile_smem, sems, *, tiles
):
    devices = first_ref.shape[0] // FIRST
    read_tiles(first_ref, tile_vmem, tile_smem, sems.at[0])
    pad_list(list_ref, list_slots(tile_smem, 0, list_ref, 0), tiles)
    pad_list(rest_ref, list_slots(tile_smem, 1, rest_ref, 0), devices * MARKS + tiles)
    end = list_slots(tile_smem, 0, all_ref, 0)
    pad_list(all_ref, list_slots(tile_smem, 1, all_ref, end), None)
    weigh_slots(first_ref, FIRST, weight_ref, 0, devices)
    keep_weights = pltpu.make_async_copy(weight_ref, weight_hbm, sems.at[1])
    keep_weights.start()

    def force_rows(slot, idx):
        return first_ref, slot * FIRST + 16 + idx

    spread_blocks(list_ref, weight_ref, force_rows, acc_ref, wide_ref, tiles, acc_ref.shape[1])
    keep_acc = pltpu.make_async_copy(acc_ref, acc_hbm, sems.at[2])
    keep_acc.start()
    keep_weights.wait()
    keep_acc.wait()


def spread_rest_kernel(
    first_ref, rest_ref, list_ref, before_hbm, weight_first_hbm, velocity_hbm,
    forced_ref, weight_ref, xlo_ref, xhi_ref, ylo_ref, yhi_ref, velocity_ref, before_ref, acc_ref, wide_ref, sems,
):
    fetches = [
        pltpu.make_async_copy(velocity_hbm, velocity_ref, sems.at[0]),
        pltpu.make_async_copy(before_hbm, before_ref, sems.at[1]),
        pltpu.make_async_copy(weight_first_hbm, weight_ref.at[0 : weight_first_hbm.shape[0]], sems.at[2]),
    ]
    for fetch in fetches:
        fetch.start()
    depth = velocity_ref.shape[3]
    size_x, size_y = velocity_ref.shape[1:3]
    tiles_y = size_y // TY
    tiles = (size_x // TX) * tiles_y
    devices = first_ref.shape[0] // FIRST
    tile_rows = 3 * TX * TY
    weigh_slots(rest_ref, REST, weight_ref, devices, devices)

    def force_rows(slot, idx):
        device = slot - devices
        if idx < 2:
            return first_ref, device * FIRST + 6 + idx
        return rest_ref, device * REST + (6 if idx < 4 else 14) + idx % 2

    spread_blocks(list_ref, weight_ref, force_rows, acc_ref, wide_ref, tiles, depth)
    for fetch in fetches:
        fetch.wait()

    def finish(x, carry):
        for c in range(3):
            for ty in range(tiles_y):
                row = ((x // TX) * tiles_y + ty) * tile_rows + c * TX * TY + (x % TX) * TY
                here = (c, x, slice(ty * TY, (ty + 1) * TY), slice(None))
                rows = pl.ds(pl.multiple_of(row, 8), TY)
                value = velocity_ref[here] + time_step * (before_ref[rows, :] + acc_ref[rows, :])
                forced_ref[here] = value
                if ty == 0:
                    ylo_ref[c, pl.ds(x, 1), :] = value[0:1, :]
                if ty == tiles_y - 1:
                    yhi_ref[c, pl.ds(x, 1), :] = value[TY - 1 : TY, :]
        return carry

    lax.fori_loop(0, size_x, finish, 0)
    xlo_ref[...] = forced_ref[:, 0]
    xhi_ref[...] = forced_ref[:, size_x - 1]


def spread_params():
    return pltpu.CompilerParams(vmem_limit_bytes=20 << 20)


def spread_first(first, tiles, depth):
    devices = first.shape[0] // FIRST
    return pl.pallas_call(
        lambda *refs: spread_first_kernel(*refs, tiles=tiles),
        out_shape=(
            pltpu.HBM(((tiles + 1) * 3 * TX * TY, depth), jnp.float32),
            pltpu.HBM((devices * WROWS, 128), jnp.float32),
            jax.ShapeDtypeStruct((devices + LIST_SPARE,), jnp.int32),
            jax.ShapeDtypeStruct((2 * devices + LIST_SPARE,), jnp.int32),
        ),
        in_specs=[VMEM],
        out_specs=(HBM, HBM, SMEM, SMEM),
        scratch_shapes=[
            pltpu.VMEM(((tiles + 1) * 3 * TX * TY, depth), jnp.float32),
            pltpu.VMEM((devices * WROWS, 128), jnp.float32),
            pltpu.VMEM((2 * UNROLL * TX, 128), jnp.float32),
            pltpu.SMEM((devices + LIST_SPARE,), jnp.int32),
            pltpu.VMEM((2, devices), jnp.int32),
            pltpu.SMEM((2, devices), jnp.int32),
            pltpu.SemaphoreType.DMA((3,)),
        ],
        compiler_params=spread_params(),
        cost_estimate=pl.CostEstimate(flops=6 << 30, transcendentals=0, bytes_accessed=16 << 20),
        name="spread_first",
    )(first)


def spread_rest(first, rest, rest_list, before, weight_first, velocity):
    _, size_x, size_y, depth = velocity.shape
    devices = first.shape[0] // FIRST
    x_face = jax.ShapeDtypeStruct((3, size_y, depth), jnp.float32)
    y_face = jax.ShapeDtypeStruct((3, size_x, depth), jnp.float32)
    return pl.pallas_call(
        spread_rest_kernel,
        out_shape=(
            jax.ShapeDtypeStruct(velocity.shape, jnp.float32),
            jax.ShapeDtypeStruct((2 * devices * WROWS, 128), jnp.float32),
            x_face,
            x_face,
            y_face,
            y_face,
        ),
        in_specs=[VMEM, VMEM, SMEM, HBM, HBM, HBM],
        out_specs=(VMEM,) * 6,
        scratch_shapes=[
            pltpu.VMEM(velocity.shape, jnp.float32),
            pltpu.VMEM(before.shape, jnp.float32),
            pltpu.VMEM(before.shape, jnp.float32),
            pltpu.VMEM((2 * UNROLL * TX, 128), jnp.float32),
            pltpu.SemaphoreType.DMA((3,)),
        ],
        compiler_params=spread_params(),
        name="spread_rest",
    )(first, rest, rest_list, before, weight_first, velocity)


def sweep_kernel(
    list_ref, weight_ref, forced_ref, xlo_ref, xhi_ref, ylo_ref, yhi_ref, next_hbm, reply_ref,
    next_ref, pad_ref, tiled_ref, wide_ref, sem,
):
    _, size_x, size_y, depth = forced_ref.shape
    tiles_y = size_y // TY
    tiles = (size_x // TX) * tiles_y
    steps = list_ref[list_ref.shape[0] - 1]
    pad_ref[:, 1 : size_x + 1, 8 : size_y + 8, :] = forced_ref[...]
    pad_ref[:, 0, 8 : size_y + 8, :] = xlo_ref[...]
    pad_ref[:, size_x + 1, 8 : size_y + 8, :] = xhi_ref[...]
    pad_ref[:, 1 : size_x + 1, 7, :] = ylo_ref[...]
    pad_ref[:, 1 : size_x + 1, size_y + 8, :] = yhi_ref[...]
    lane = lax.broadcasted_iota(jnp.int32, (TY, depth), 1)
    first_lane, last_lane = lane == 0, lane == depth - 1

    def column(x2, carry):
        for ty in range(tiles_y):
            y0 = 8 + ty * TY
            halves = [[], [], []]
            for dx in range(2):
                x = x2 * 2 + dx + 1
                centre = [pad_ref[c, x, y0 : y0 + TY, :] for c in range(3)]
                for c in range(3):
                    plus_x = pad_ref[c, x + 1, y0 : y0 + TY, :]
                    minus_x = pad_ref[c, x - 1, y0 : y0 + TY, :]
                    plus_y = pad_ref[c, x, y0 + 1 : y0 + TY + 1, :]
                    minus_y = pad_ref[c, x, y0 - 1 : y0 + TY - 1, :]
                    plus_z = jnp.where(last_lane, 0.0, pltpu.roll(centre[c], depth - 1, 1))
                    minus_z = jnp.where(first_lane, 0.0, pltpu.roll(centre[c], 1, 1))
                    laplace = plus_x + minus_x + plus_y + minus_y + plus_z + minus_z - 6.0 * centre[c]
                    advect = (
                        centre[0] * (plus_x - minus_x)
                        + centre[1] * (plus_y - minus_y)
                        + centre[2] * (plus_z - minus_z)
                    ) * 0.5
                    value = centre[c] + time_step * (viscosity * laplace - advect)
                    next_ref[c, x - 1, ty * TY : (ty + 1) * TY, :] = value
                    halves[c].append(value)
            tile = (x2 // (TX // 2)) * tiles_y + ty
            for c in range(3):
                row = pl.multiple_of((tile * 3 + c) * (TX * TY) + (x2 % (TX // 2)) * 16, 16)
                tiled_ref[pl.ds(row, 16), :] = jnp.concatenate(halves[c], axis=0).astype(jnp.bfloat16)
        return carry

    lax.fori_loop(0, size_x // 2, column, 0)
    store = pltpu.make_async_copy(next_ref, next_hbm, sem)
    store.start()

    table = cell_table()

    def build(slot, mark, k):
        to = pl.multiple_of(slot * WROWS, 8)
        along_z = []
        for q in range(2):
            wx = weights_x(weight_ref, to, q, table)
            at = (2 * k + q) * TX
            for part in range(TX // 8):
                wide_ref[at + part * 8 : at + part * 8 + 8, :] = wx[part]
            along_z.append(jnp.concatenate(weights_z(weight_ref, to, q, depth, table), axis=0))
        row = pl.multiple_of(mark * (3 * TX * TY), 16)
        return lax.dot_general(
            tiled_ref[pl.ds(row, 3 * TX * TY), :],
            jnp.concatenate(along_z, axis=1),
            (((1,), (0,)), ((), ())),
            preferred_element_type=jnp.float32,
        )

    devices = weight_ref.shape[0] // (2 * WROWS)

    def finish(slot, along, k):
        to = pl.multiple_of(slot * WROWS, 8)
        rank = (slot >= devices).astype(jnp.int32)
        device = slot - rank * devices
        for q in range(2):
            at = (2 * k + q) * TX
            sums = [None] * 3
            for i in range(TX):
                weight = wide(wide_ref, at + i)
                for c in range(3):
                    row = c * TX * TY + i * TY
                    term = weight * along[row : row + TY, q * 128 : (q + 1) * 128]
                    sums[c] = term if sums[c] is None else sums[c] + term
            wy = weights_y(weight_ref, to, q, table)
            for c in range(3):
                result = jnp.sum(sums[c] * wy, axis=0, keepdims=True)
                reply_ref[device * 3 + c, pl.ds(2 * rank + q, 1), :] = result

    def step(n, carry):
        codes = [list_ref[UNROLL * n + k] for k in range(UNROLL)]
        outs = [build(lax.shift_right_logical(code, MARK_BITS), code & (MARKS - 1), k) for k, code in enumerate(codes)]
        for k, code in enumerate(codes):
            finish(lax.shift_right_logical(code, MARK_BITS), outs[k], k)
        return carry

    lax.fori_loop(0, steps, step, 0)
    store.wait()


def sweep(slot_list, weights, forced, xlo, xhi, ylo, yhi):
    smem = pl.BlockSpec(memory_space=pltpu.SMEM)
    vmem = pl.BlockSpec(memory_space=pltpu.VMEM)
    _, size_x, size_y, depth = forced.shape
    devices = weights.shape[0] // (2 * WROWS)
    return pl.pallas_call(
        sweep_kernel,
        out_shape=(
            jax.ShapeDtypeStruct(forced.shape, jnp.float32),
            jax.ShapeDtypeStruct((devices * 3, 4, 128), jnp.float32),
        ),
        in_specs=[smem] + [vmem] * 6,
        out_specs=(HBM, vmem),
        scratch_shapes=[
            pltpu.VMEM(forced.shape, jnp.float32),
            pltpu.VMEM((3, size_x + 2, size_y + 16, depth), jnp.float32),
            pltpu.VMEM((3 * size_x * size_y, depth), jnp.bfloat16),
            pltpu.VMEM((2 * UNROLL * TX, 128), jnp.float32),
            pltpu.SemaphoreType.DMA,
        ],
        compiler_params=pltpu.CompilerParams(vmem_limit_bytes=24 << 20),
        name="sweep",
    )(slot_list, weights, forced, xlo, xhi, ylo, yhi)


def gather_kernel(slot_ref, back_ref, out_ref):
    blocks = out_ref.shape[1]

    def take(group, carry):
        b0 = pl.multiple_of(group * 8, 8)
        slots = [slot_ref[b0 + j] for j in range(8)]
        for q in range(2):
            for c in range(3):
                rows = [back_ref[lax.shift_right_logical(slot, 1) * 3 + c, pl.ds((slot & 1) * 2 + q, 1), :] for slot in slots]
                out_ref[c, pl.ds(b0, 8), q * 128 : (q + 1) * 128] = jnp.concatenate(rows, axis=0)
        return carry

    lax.fori_loop(0, blocks // 8, take, 0)


def gather(slot, back):
    smem = pl.BlockSpec(memory_space=pltpu.SMEM)
    vmem = pl.BlockSpec(memory_space=pltpu.VMEM)
    return pl.pallas_call(
        gather_kernel,
        out_shape=jax.ShapeDtypeStruct((3, slot.shape[0], 256), jnp.float32),
        in_specs=[smem, vmem],
        out_specs=vmem,
        name="gather",
    )(slot, back)


def neighbour(value, axis, step):
    count = lax.axis_size(axis)
    return lax.ppermute(value, axis, [(i, i + step) for i in range(count) if 0 <= i + step < count])


def exchange(rows, devices):
    shaped = rows.reshape((devices, rows.shape[0] // devices) + rows.shape[1:])
    return lax.all_to_all(shaped, AXES, split_axis=0, concat_axis=0, tiled=True).reshape(rows.shape)


def body(velocity, forces, offsets, base_x, base_y, base_z, home_device, home_tile):
    devices = lax.axis_size("gx") * lax.axis_size("gy")
    _, size_x, size_y, depth = velocity.shape
    tiles = (size_x // TX) * (size_y // TY)
    send_first, send_rest, slot = pack(
        home_device[:, 0],
        home_tile,
        jnp.transpose(forces, (1, 0, 2)),
        jnp.transpose(offsets, (1, 0, 2)),
        base_x,
        base_y,
        base_z,
        devices,
    )
    first = exchange(send_first, devices)
    rest = exchange(send_rest, devices)
    before, weight_first, rest_list, all_list = spread_first(first, tiles, depth)
    before, weight_first, velocity = (
        pltpu.with_memory_space_constraint(x, pltpu.HBM) for x in (before, weight_first, velocity)
    )
    forced, weights, x_first, x_last, y_first, y_last = spread_rest(
        first, rest, rest_list, before, weight_first, velocity
    )
    xlo = neighbour(x_last, "gx", 1)
    xhi = neighbour(x_first, "gx", -1)
    ylo = neighbour(y_last, "gy", 1)
    yhi = neighbour(y_first, "gy", -1)
    velocity_next, reply = sweep(all_list, weights, forced, xlo, xhi, ylo, yhi)
    back = exchange(reply, devices)
    fibre = gather(slot, back)
    return velocity_next, jnp.transpose(fibre, (1, 0, 2))


def solution(mesh):
    return jax.shard_map(
        body,
        mesh=mesh,
        in_specs=(
            P(None, "gx", "gy", None),
            P(AXES, None, None),
            P(AXES, None, None),
            P(AXES, None),
            P(AXES, None),
            P(AXES, None),
            P(AXES, None),
            P(AXES),
        ),
        out_specs=(P(None, "gx", "gy", None), P(AXES, None, None)),
        check_vma=False,
    )
```

```python
import jax
import jax.numpy as jnp
from jax import lax
from jax.experimental import pallas as pl
from jax.experimental.pallas import tpu as pltpu
from jax.sharding import PartitionSpec as P

TX = 16
TY = 8
FIRST = 24
REST = 16
MARK_BITS = 5
MARKS = 1 << MARK_BITS
WROWS = 40
UNROLL = 16
LIST_SPARE = UNROLL + 8
AXES = ("gx", "gy")

SMEM = pl.BlockSpec(memory_space=pltpu.SMEM)
VMEM = pl.BlockSpec(memory_space=pltpu.VMEM)
HBM = pl.BlockSpec(memory_space=pltpu.HBM)

time_step = 0.4
viscosity = 0.15
spread_rate = time_step * viscosity


def pack_kernel(home_ref, tile_ref, forces_ref, offsets_ref, bx_ref, by_ref, bz_ref, first_ref, rest_ref, slot_ref, count_ref):
    blocks = forces_ref.shape[1]
    devices = first_ref.shape[0] // FIRST

    def clear(d, carry):
        count_ref[d] = 0
        first_ref[pl.ds(d * FIRST + 14, 2), :] = jnp.full((2, 128), -1.0, jnp.float32)
        return carry

    lax.fori_loop(0, devices, clear, 0, unroll=8)

    def put(send_ref, start, rows, forces, values):
        offsets, bases, force = values
        for idx in range(6):
            send_ref[pl.ds(start + idx, 1), :] = offsets[idx]
            send_ref[pl.ds(start + 8 + idx, 1), :] = bases[idx]
        for idx in forces:
            send_ref[pl.ds(start + rows[idx], 1), :] = force[idx]

    def place(group, carry):
        b0 = pl.multiple_of(group * 8, 8)
        offsets, bases, forces = [], [], []
        for q in range(2):
            lanes = slice(q * 128, (q + 1) * 128)
            for v in range(3):
                offsets.append(offsets_ref[v, pl.ds(b0, 8), lanes])
                bases.append((bx_ref, by_ref, bz_ref)[v][pl.ds(b0, 8), lanes].astype(jnp.float32))
                forces.append(forces_ref[v, pl.ds(b0, 8), lanes])
        for j in range(8):
            home = home_ref[b0 + j]
            rank = count_ref[home]
            count_ref[home] = rank + 1
            slot_ref[b0 + j] = home * 2 + rank
            mark = jnp.full((1, 128), tile_ref[b0 + j].astype(jnp.float32), jnp.float32)
            first_ref[pl.ds(home * FIRST + 14 + rank, 1), :] = mark
            values = [[x[j : j + 1, :] for x in group] for group in (offsets, bases, forces)]

            @pl.when(rank == 0)
            def _():
                put(first_ref, home * FIRST, range(16, 22), range(6), values)

            @pl.when(rank != 0)
            def _():
                put(rest_ref, home * REST, (None, None, 6, 7, 14, 15), range(2, 6), values)
                for idx in range(2):
                    first_ref[pl.ds(home * FIRST + 6 + idx, 1), :] = values[2][idx]

        return carry

    lax.fori_loop(0, blocks // 8, place, 0)


def pack(home, tile, forces, offsets, bx, by, bz, devices):
    blocks = home.shape[0]
    return pl.pallas_call(
        pack_kernel,
        out_shape=(
            pltpu.VMEM((devices * FIRST, 128), jnp.float32),
            pltpu.VMEM((devices * REST, 128), jnp.float32),
            jax.ShapeDtypeStruct((blocks,), jnp.int32),
        ),
        in_specs=[SMEM, SMEM] + [VMEM] * 5,
        out_specs=(VMEM, VMEM, SMEM),
        scratch_shapes=[pltpu.SMEM((devices,), jnp.int32)],
        name="pack",
    )(home, tile, forces, offsets, bx, by, bz)


def read_tiles(first_ref, tile_vmem, tile_smem, sem):
    devices = first_ref.shape[0] // FIRST
    lane = lax.broadcasted_iota(jnp.int32, (2, devices), 1)
    rank = lax.broadcasted_iota(jnp.int32, (2, devices), 0)
    found = jnp.full((2, devices), -1.0, jnp.float32)
    for d in range(devices):
        found = jnp.where(lane == d, first_ref[d * FIRST + 14 : d * FIRST + 16, :], found)
    tile = found.astype(jnp.int32)
    tile_vmem[...] = jnp.where(tile < 0, -1, (rank * devices + lane) * MARKS + tile)
    copy = pltpu.make_async_copy(tile_vmem, tile_smem, sem)
    copy.start()
    copy.wait()


def list_slots(tile_smem, rank, list_ref, start):
    def step(d, n):
        code = tile_smem[rank, d]
        list_ref[n] = code
        return n + 1 + lax.shift_right_arithmetic(code, 31)

    return lax.fori_loop(0, tile_smem.shape[1], step, start, unroll=16)


def pad_list(list_ref, end, spare):
    last = list_ref[jnp.maximum(end - 1, 0)]
    for extra in range(UNROLL - 1):
        list_ref[end + extra] = last if spare is None else spare
    list_ref[list_ref.shape[0] - 1] = (end + UNROLL - 1) // UNROLL


def weigh_slots(recv_ref, stride, weight_ref, first, devices):
    row = lax.broadcasted_iota(jnp.int32, (8, 128), 0)
    along_z = (row == 2) | (row == 5)

    def one(device):
        start = pl.multiple_of(device * stride, 8)
        off = recv_ref[pl.ds(start, 8), :]
        base = recv_ref[pl.ds(start + 8, 8), :]
        square = 1.0 + 4.0 * off - 4.0 * off * off
        rad = square * lax.rsqrt(square)
        low, high = 3.0 - 2.0 * off, 1.0 + 2.0 * off
        block = jnp.floor(base * 0.0625)
        to = pl.multiple_of((first + device) * WROWS, 8)
        weight_ref[pl.ds(to, 8), :] = jnp.where(along_z, base - 16.0 * block, base)
        weight_ref[pl.ds(to + 6, 1), :] = block[2:3, :]
        weight_ref[pl.ds(to + 7, 1), :] = block[5:6, :]
        weight_ref[pl.ds(to + 8, 8), :] = (low - rad) * 0.125
        weight_ref[pl.ds(to + 16, 8), :] = (low + rad) * 0.125
        weight_ref[pl.ds(to + 24, 8), :] = (high + rad) * 0.125
        weight_ref[pl.ds(to + 32, 8), :] = (high - rad) * 0.125

    def four(n, carry):
        for k in range(4):
            one(n * 4 + k)
        return carry

    lax.fori_loop(0, devices // 4, four, 0)


def wide(ref, row, dtype=jnp.float32):
    value = ref[pl.ds(row, 8, stride=0), :]
    if dtype == jnp.float32:
        return value
    return jnp.concatenate([value, value], axis=0).astype(dtype)


def picked(base, weights, cells):
    out = jnp.zeros(base.shape, base.dtype)
    for weight, cell in zip(weights, cells):
        out = jnp.where(base == cell, weight, out)
    return out


def cells_from(first, sublanes, dtype):
    cell = lax.broadcasted_iota(jnp.int32, (sublanes, 128), 0) + first
    return cell.astype(jnp.float32).astype(dtype)


def cell_table():
    f32, half = jnp.float32, jnp.bfloat16
    table = {(n, f32): cells_from(n, 8, f32) for n in range(-3, 9)}
    table.update({(n, half): cells_from(n, 16, half) for n in (-3, -2, -1, 0, 13, 14, 15)})
    return table


def weights_x(weight_ref, to, q, table):
    base = wide(weight_ref, to + q * 3)
    ws = [wide(weight_ref, to + 8 + 8 * m + q * 3) for m in range(4)]
    return [picked(base, ws, [table[8 * k - m, jnp.float32] for m in range(4)]) for k in range(TX // 8)]


def weights_y(weight_ref, to, q, table):
    base = wide(weight_ref, to + q * 3 + 1)
    ws = [wide(weight_ref, to + 8 + 8 * m + q * 3 + 1) for m in range(4)]
    return picked(base, ws, [table[-m, jnp.float32] for m in range(4)])


def weights_z(weight_ref, to, q, depth, table):
    half = jnp.bfloat16
    base = wide(weight_ref, to + q * 3 + 2, half)
    block = wide(weight_ref, to + 6 + q, half)
    ws = [wide(weight_ref, to + 8 + 8 * m + q * 3 + 2, half) for m in range(4)]
    low = picked(base, ws, [table[-m, half] for m in range(4)])
    high = picked(base, ws[1:], [table[16 - m, half] for m in range(1, 4)])
    zero = jnp.zeros((16, 128), half)
    here = [block == jnp.full((16, 128), k, half) for k in range(depth // 16)]
    out = []
    for k in range(depth // 16):
        before = jnp.where(here[k - 1], high, zero) if k else zero
        out.append(jnp.where(here[k], low, before))
    return out


def spread_blocks(list_ref, weight_ref, force_rows, acc_ref, wide_ref, tiles, depth):
    tile_rows = 3 * TX * TY

    def clear(n, carry):
        acc_ref[pl.ds(pl.multiple_of(n * tile_rows, 8), tile_rows), :] = jnp.zeros((tile_rows, depth), jnp.float32)
        return carry

    lax.fori_loop(0, tiles, clear, 0)
    table = cell_table()

    def build(slot, k):
        to = pl.multiple_of(slot * WROWS, 8)
        kernel_xy, weighted = [], []
        for q in range(2):
            wx = weights_x(weight_ref, to, q, table)
            at = (2 * k + q) * TX
            for part in range(TX // 8):
                wide_ref[at + part * 8 : at + part * 8 + 8, :] = wx[part]
            wy = weights_y(weight_ref, to, q, table)
            columns = [wide(wide_ref, at + i) * wy for i in range(TX)]
            kernel_xy.append(jnp.concatenate(columns, axis=0).astype(jnp.bfloat16))
            wz = weights_z(weight_ref, to, q, depth, table)
            parts = []
            for c in range(3):
                force = wide(*force_rows(slot, q * 3 + c), jnp.bfloat16)
                parts += [w * force for w in wz]
            weighted.append(jnp.concatenate(parts, axis=0))
        return lax.dot_general(
            jnp.concatenate(kernel_xy, axis=1),
            jnp.concatenate(weighted, axis=1),
            (((1,), (1,)), ((), ())),
            preferred_element_type=jnp.float32,
        )

    def add(tile, out):
        for c in range(3):
            here = pl.ds(pl.multiple_of(tile * tile_rows + c * TX * TY, 8), TX * TY)
            acc_ref[here, :] = acc_ref[here, :] + out[:, c * depth : (c + 1) * depth]

    def step(n, carry):
        codes = [list_ref[UNROLL * n + k] for k in range(UNROLL)]
        outs = [build(lax.shift_right_logical(code, MARK_BITS), k) for k, code in enumerate(codes)]
        for code, out in zip(codes, outs):
            add(code & (MARKS - 1), out)
        return carry

    lax.fori_loop(0, list_ref[list_ref.shape[0] - 1], step, 0)


def spread_first_kernel(
    first_ref, acc_hbm, weight_hbm, rest_ref, all_ref,
    acc_ref, weight_ref, wide_ref, list_ref, tile_vmem, tile_smem, sems, *, tiles
):
    devices = first_ref.shape[0] // FIRST
    read_tiles(first_ref, tile_vmem, tile_smem, sems.at[0])
    pad_list(list_ref, list_slots(tile_smem, 0, list_ref, 0), tiles)
    pad_list(rest_ref, list_slots(tile_smem, 1, rest_ref, 0), devices * MARKS + tiles)
    end = list_slots(tile_smem, 0, all_ref, 0)
    pad_list(all_ref, list_slots(tile_smem, 1, all_ref, end), None)
    weigh_slots(first_ref, FIRST, weight_ref, 0, devices)
    keep_weights = pltpu.make_async_copy(weight_ref, weight_hbm, sems.at[1])
    keep_weights.start()

    def force_rows(slot, idx):
        return first_ref, slot * FIRST + 16 + idx

    spread_blocks(list_ref, weight_ref, force_rows, acc_ref, wide_ref, tiles, acc_ref.shape[1])
    keep_acc = pltpu.make_async_copy(acc_ref, acc_hbm, sems.at[2])
    keep_acc.start()
    keep_weights.wait()
    keep_acc.wait()


def spread_rest_kernel(
    first_ref, rest_ref, list_ref, before_hbm, weight_first_hbm, velocity_hbm,
    forced_ref, weight_ref, xlo_ref, xhi_ref, ylo_ref, yhi_ref, velocity_ref, before_ref, acc_ref, wide_ref, sems,
):
    fetches = [
        pltpu.make_async_copy(velocity_hbm, velocity_ref, sems.at[0]),
        pltpu.make_async_copy(before_hbm, before_ref, sems.at[1]),
        pltpu.make_async_copy(weight_first_hbm, weight_ref.at[0 : weight_first_hbm.shape[0]], sems.at[2]),
    ]
    for fetch in fetches:
        fetch.start()
    depth = velocity_ref.shape[3]
    size_x, size_y = velocity_ref.shape[1:3]
    tiles_y = size_y // TY
    tiles = (size_x // TX) * tiles_y
    devices = first_ref.shape[0] // FIRST
    tile_rows = 3 * TX * TY
    weigh_slots(rest_ref, REST, weight_ref, devices, devices)

    def force_rows(slot, idx):
        device = slot - devices
        if idx < 2:
            return first_ref, device * FIRST + 6 + idx
        return rest_ref, device * REST + (6 if idx < 4 else 14) + idx % 2

    spread_blocks(list_ref, weight_ref, force_rows, acc_ref, wide_ref, tiles, depth)
    for fetch in fetches:
        fetch.wait()

    def finish(x, carry):
        for c in range(3):
            for ty in range(tiles_y):
                row = ((x // TX) * tiles_y + ty) * tile_rows + c * TX * TY + (x % TX) * TY
                here = (c, x, slice(ty * TY, (ty + 1) * TY), slice(None))
                rows = pl.ds(pl.multiple_of(row, 8), TY)
                value = velocity_ref[here] + time_step * (before_ref[rows, :] + acc_ref[rows, :])
                forced_ref[here] = value
                if ty == 0:
                    ylo_ref[c, pl.ds(x, 1), :] = value[0:1, :]
                if ty == tiles_y - 1:
                    yhi_ref[c, pl.ds(x, 1), :] = value[TY - 1 : TY, :]
        return carry

    lax.fori_loop(0, size_x, finish, 0, unroll=4)
    xlo_ref[...] = forced_ref[:, 0]
    xhi_ref[...] = forced_ref[:, size_x - 1]


def spread_params():
    return pltpu.CompilerParams(vmem_limit_bytes=20 << 20)


def spread_first(first, tiles, depth):
    devices = first.shape[0] // FIRST
    return pl.pallas_call(
        lambda *refs: spread_first_kernel(*refs, tiles=tiles),
        out_shape=(
            pltpu.HBM(((tiles + 1) * 3 * TX * TY, depth), jnp.float32),
            pltpu.HBM((devices * WROWS, 128), jnp.float32),
            jax.ShapeDtypeStruct((devices + LIST_SPARE,), jnp.int32),
            jax.ShapeDtypeStruct((2 * devices + LIST_SPARE,), jnp.int32),
        ),
        in_specs=[VMEM],
        out_specs=(HBM, HBM, SMEM, SMEM),
        scratch_shapes=[
            pltpu.VMEM(((tiles + 1) * 3 * TX * TY, depth), jnp.float32),
            pltpu.VMEM((devices * WROWS, 128), jnp.float32),
            pltpu.VMEM((2 * UNROLL * TX, 128), jnp.float32),
            pltpu.SMEM((devices + LIST_SPARE,), jnp.int32),
            pltpu.VMEM((2, devices), jnp.int32),
            pltpu.SMEM((2, devices), jnp.int32),
            pltpu.SemaphoreType.DMA((3,)),
        ],
        compiler_params=spread_params(),
        cost_estimate=pl.CostEstimate(flops=6 << 30, transcendentals=0, bytes_accessed=16 << 20),
        name="spread_first",
    )(first)


def spread_rest(first, rest, rest_list, before, weight_first, velocity):
    _, size_x, size_y, depth = velocity.shape
    devices = first.shape[0] // FIRST
    x_face = jax.ShapeDtypeStruct((3, size_y, depth), jnp.float32)
    y_face = jax.ShapeDtypeStruct((3, size_x, depth), jnp.float32)
    return pl.pallas_call(
        spread_rest_kernel,
        out_shape=(
            jax.ShapeDtypeStruct(velocity.shape, jnp.float32),
            jax.ShapeDtypeStruct((2 * devices * WROWS, 128), jnp.float32),
            x_face,
            x_face,
            y_face,
            y_face,
        ),
        in_specs=[VMEM, VMEM, SMEM, HBM, HBM, HBM],
        out_specs=(VMEM,) * 6,
        scratch_shapes=[
            pltpu.VMEM(velocity.shape, jnp.float32),
            pltpu.VMEM(before.shape, jnp.float32),
            pltpu.VMEM(before.shape, jnp.float32),
            pltpu.VMEM((2 * UNROLL * TX, 128), jnp.float32),
            pltpu.SemaphoreType.DMA((3,)),
        ],
        compiler_params=spread_params(),
        name="spread_rest",
    )(first, rest, rest_list, before, weight_first, velocity)


def sweep_kernel(
    list_ref, weight_ref, forced_ref, xlo_ref, xhi_ref, ylo_ref, yhi_ref, next_hbm, reply_ref,
    next_ref, pad_ref, tiled_ref, wide_ref, sem,
):
    _, size_x, size_y, depth = forced_ref.shape
    tiles_y = size_y // TY
    tiles = (size_x // TX) * tiles_y
    steps = list_ref[list_ref.shape[0] - 1]
    pad_ref[:, 1 : size_x + 1, 8 : size_y + 8, :] = forced_ref[...]
    pad_ref[:, 0, 8 : size_y + 8, :] = xlo_ref[...]
    pad_ref[:, size_x + 1, 8 : size_y + 8, :] = xhi_ref[...]
    pad_ref[:, 1 : size_x + 1, 7, :] = ylo_ref[...]
    pad_ref[:, 1 : size_x + 1, size_y + 8, :] = yhi_ref[...]
    lane = lax.broadcasted_iota(jnp.int32, (TY, depth), 1)
    first_lane, last_lane = lane == 0, lane == depth - 1

    def column(x2, carry):
        for ty in range(tiles_y):
            y0 = 8 + ty * TY
            halves = [[], [], []]
            for dx in range(2):
                x = x2 * 2 + dx + 1
                centre = [pad_ref[c, x, y0 : y0 + TY, :] for c in range(3)]
                drift = [(0.5 * time_step) * u for u in centre]
                ahead = [spread_rate - d for d in drift]
                behind = [spread_rate + d for d in drift]
                ahead[2] = jnp.where(last_lane, 0.0, ahead[2])
                behind[2] = jnp.where(first_lane, 0.0, behind[2])
                for c in range(3):
                    value = (
                        (1.0 - 6.0 * spread_rate) * centre[c]
                        + ahead[0] * pad_ref[c, x + 1, y0 : y0 + TY, :]
                        + behind[0] * pad_ref[c, x - 1, y0 : y0 + TY, :]
                        + ahead[1] * pad_ref[c, x, y0 + 1 : y0 + TY + 1, :]
                        + behind[1] * pad_ref[c, x, y0 - 1 : y0 + TY - 1, :]
                        + ahead[2] * pltpu.roll(centre[c], depth - 1, 1)
                        + behind[2] * pltpu.roll(centre[c], 1, 1)
                    )
                    next_ref[c, x - 1, ty * TY : (ty + 1) * TY, :] = value
                    halves[c].append(value)
            tile = (x2 // (TX // 2)) * tiles_y + ty
            for c in range(3):
                row = pl.multiple_of((tile * 3 + c) * (TX * TY) + (x2 % (TX // 2)) * 16, 16)
                tiled_ref[pl.ds(row, 16), :] = jnp.concatenate(halves[c], axis=0).astype(jnp.bfloat16)
        return carry

    lax.fori_loop(0, size_x // 2, column, 0)
    store = pltpu.make_async_copy(next_ref, next_hbm, sem)
    store.start()

    table = cell_table()

    def build(slot, mark, k):
        to = pl.multiple_of(slot * WROWS, 8)
        along_z = []
        for q in range(2):
            wx = weights_x(weight_ref, to, q, table)
            at = (2 * k + q) * TX
            for part in range(TX // 8):
                wide_ref[at + part * 8 : at + part * 8 + 8, :] = wx[part]
            along_z.append(jnp.concatenate(weights_z(weight_ref, to, q, depth, table), axis=0))
        row = pl.multiple_of(mark * (3 * TX * TY), 16)
        return lax.dot_general(
            tiled_ref[pl.ds(row, 3 * TX * TY), :],
            jnp.concatenate(along_z, axis=1),
            (((1,), (0,)), ((), ())),
            preferred_element_type=jnp.float32,
        )

    devices = weight_ref.shape[0] // (2 * WROWS)

    def finish(slot, along, k):
        to = pl.multiple_of(slot * WROWS, 8)
        rank = (slot >= devices).astype(jnp.int32)
        device = slot - rank * devices
        for q in range(2):
            at = (2 * k + q) * TX
            sums = [None] * 3
            for i in range(TX):
                weight = wide(wide_ref, at + i)
                for c in range(3):
                    row = c * TX * TY + i * TY
                    term = weight * along[row : row + TY, q * 128 : (q + 1) * 128]
                    sums[c] = term if sums[c] is None else sums[c] + term
            wy = weights_y(weight_ref, to, q, table)
            for c in range(3):
                result = jnp.sum(sums[c] * wy, axis=0, keepdims=True)
                reply_ref[device * 3 + c, pl.ds(2 * rank + q, 1), :] = result

    def step(n, carry):
        codes = [list_ref[UNROLL * n + k] for k in range(UNROLL)]
        outs = [build(lax.shift_right_logical(code, MARK_BITS), code & (MARKS - 1), k) for k, code in enumerate(codes)]
        for k, code in enumerate(codes):
            finish(lax.shift_right_logical(code, MARK_BITS), outs[k], k)
        return carry

    lax.fori_loop(0, steps, step, 0)
    store.wait()


def sweep(slot_list, weights, forced, xlo, xhi, ylo, yhi):
    smem = pl.BlockSpec(memory_space=pltpu.SMEM)
    vmem = pl.BlockSpec(memory_space=pltpu.VMEM)
    _, size_x, size_y, depth = forced.shape
    devices = weights.shape[0] // (2 * WROWS)
    return pl.pallas_call(
        sweep_kernel,
        out_shape=(
            jax.ShapeDtypeStruct(forced.shape, jnp.float32),
            jax.ShapeDtypeStruct((devices * 3, 4, 128), jnp.float32),
        ),
        in_specs=[smem] + [vmem] * 6,
        out_specs=(HBM, vmem),
        scratch_shapes=[
            pltpu.VMEM(forced.shape, jnp.float32),
            pltpu.VMEM((3, size_x + 2, size_y + 16, depth), jnp.float32),
            pltpu.VMEM((3 * size_x * size_y, depth), jnp.bfloat16),
            pltpu.VMEM((2 * UNROLL * TX, 128), jnp.float32),
            pltpu.SemaphoreType.DMA,
        ],
        compiler_params=pltpu.CompilerParams(vmem_limit_bytes=24 << 20),
        name="sweep",
    )(slot_list, weights, forced, xlo, xhi, ylo, yhi)


def gather_kernel(slot_ref, back_ref, out_ref):
    blocks = out_ref.shape[1]

    def take(group, carry):
        b0 = pl.multiple_of(group * 8, 8)
        slots = [slot_ref[b0 + j] for j in range(8)]
        for q in range(2):
            for c in range(3):
                rows = [back_ref[lax.shift_right_logical(slot, 1) * 3 + c, pl.ds((slot & 1) * 2 + q, 1), :] for slot in slots]
                out_ref[c, pl.ds(b0, 8), q * 128 : (q + 1) * 128] = jnp.concatenate(rows, axis=0)
        return carry

    lax.fori_loop(0, blocks // 8, take, 0)


def gather(slot, back):
    smem = pl.BlockSpec(memory_space=pltpu.SMEM)
    vmem = pl.BlockSpec(memory_space=pltpu.VMEM)
    return pl.pallas_call(
        gather_kernel,
        out_shape=jax.ShapeDtypeStruct((3, slot.shape[0], 256), jnp.float32),
        in_specs=[smem, vmem],
        out_specs=vmem,
        name="gather",
    )(slot, back)


def neighbour(value, axis, step):
    count = lax.axis_size(axis)
    return lax.ppermute(value, axis, [(i, i + step) for i in range(count) if 0 <= i + step < count])


def exchange(rows, devices):
    shaped = rows.reshape((devices, rows.shape[0] // devices) + rows.shape[1:])
    return lax.all_to_all(shaped, AXES, split_axis=0, concat_axis=0, tiled=True).reshape(rows.shape)


def body(velocity, forces, offsets, base_x, base_y, base_z, home_device, home_tile):
    devices = lax.axis_size("gx") * lax.axis_size("gy")
    _, size_x, size_y, depth = velocity.shape
    tiles = (size_x // TX) * (size_y // TY)
    send_first, send_rest, slot = pack(
        home_device[:, 0],
        home_tile,
        jnp.transpose(forces, (1, 0, 2)),
        jnp.transpose(offsets, (1, 0, 2)),
        base_x,
        base_y,
        base_z,
        devices,
    )
    first = exchange(send_first, devices)
    rest = exchange(send_rest, devices)
    before, weight_first, rest_list, all_list = spread_first(first, tiles, depth)
    before = pltpu.with_memory_space_constraint(before, pltpu.HBM)
    weight_first = pltpu.with_memory_space_constraint(weight_first, pltpu.HBM)
    velocity = pltpu.with_memory_space_constraint(velocity, pltpu.HBM)
    forced, weights, x_first, x_last, y_first, y_last = spread_rest(
        first, rest, rest_list, before, weight_first, velocity
    )
    xlo = neighbour(x_last, "gx", 1)
    xhi = neighbour(x_first, "gx", -1)
    ylo = neighbour(y_last, "gy", 1)
    yhi = neighbour(y_first, "gy", -1)
    velocity_next, reply = sweep(all_list, weights, forced, xlo, xhi, ylo, yhi)
    back = pltpu.with_memory_space_constraint(exchange(reply, devices), pltpu.VMEM)
    fibre = gather(slot, back)
    return velocity_next, jnp.transpose(fibre, (1, 0, 2))


def solution(mesh):
    return jax.shard_map(
        body,
        mesh=mesh,
        in_specs=(
            P(None, "gx", "gy", None),
            P(AXES, None, None),
            P(AXES, None, None),
            P(AXES, None),
            P(AXES, None),
            P(AXES, None),
            P(AXES, None),
            P(AXES),
        ),
        out_specs=(P(None, "gx", "gy", None), P(AXES, None, None)),
        check_vma=False,
    )
```

```python
import jax
import jax.numpy as jnp
from jax import lax
from jax.experimental import pallas as pl
from jax.experimental.pallas import tpu as pltpu
from jax.sharding import PartitionSpec as P

TX = 16
TY = 8
FIRST = 24
REST = 16
MARK_BITS = 5
MARKS = 1 << MARK_BITS
WROWS = 40
UNROLL = 32
LIST_SPARE = UNROLL + 8
AXES = ("gx", "gy")

SMEM = pl.BlockSpec(memory_space=pltpu.SMEM)
VMEM = pl.BlockSpec(memory_space=pltpu.VMEM)
HBM = pl.BlockSpec(memory_space=pltpu.HBM)

time_step = 0.4
viscosity = 0.15
spread_rate = time_step * viscosity


def pack_kernel(home_ref, tile_ref, forces_ref, offsets_ref, bx_ref, by_ref, bz_ref, first_ref, rest_ref, slot_ref, count_ref):
    blocks = forces_ref.shape[1]
    devices = first_ref.shape[0] // FIRST

    def clear(d, carry):
        count_ref[d] = 0
        first_ref[pl.ds(d * FIRST + 14, 2), :] = jnp.full((2, 128), -1.0, jnp.float32)
        return carry

    lax.fori_loop(0, devices, clear, 0, unroll=8)

    def put(send_ref, start, rows, forces, values):
        offsets, bases, force = values
        for idx in range(6):
            send_ref[pl.ds(start + idx, 1), :] = offsets[idx]
            send_ref[pl.ds(start + 8 + idx, 1), :] = bases[idx]
        for idx in forces:
            send_ref[pl.ds(start + rows[idx], 1), :] = force[idx]

    def place(group, carry):
        b0 = pl.multiple_of(group * 8, 8)
        offsets, bases, forces = [], [], []
        for q in range(2):
            lanes = slice(q * 128, (q + 1) * 128)
            for v in range(3):
                offsets.append(offsets_ref[v, pl.ds(b0, 8), lanes])
                bases.append((bx_ref, by_ref, bz_ref)[v][pl.ds(b0, 8), lanes].astype(jnp.float32))
                forces.append(forces_ref[v, pl.ds(b0, 8), lanes])
        for j in range(8):
            home = home_ref[b0 + j]
            rank = count_ref[home]
            count_ref[home] = rank + 1
            slot_ref[b0 + j] = home * 2 + rank
            mark = jnp.full((1, 128), tile_ref[b0 + j].astype(jnp.float32), jnp.float32)
            first_ref[pl.ds(home * FIRST + 14 + rank, 1), :] = mark
            values = [[x[j : j + 1, :] for x in group] for group in (offsets, bases, forces)]

            @pl.when(rank == 0)
            def _():
                put(first_ref, home * FIRST, range(16, 22), range(6), values)

            @pl.when(rank != 0)
            def _():
                put(rest_ref, home * REST, (None, None, 6, 7, 14, 15), range(2, 6), values)
                for idx in range(2):
                    first_ref[pl.ds(home * FIRST + 6 + idx, 1), :] = values[2][idx]

        return carry

    lax.fori_loop(0, blocks // 8, place, 0)


def pack(home, tile, forces, offsets, bx, by, bz, devices):
    blocks = home.shape[0]
    return pl.pallas_call(
        pack_kernel,
        out_shape=(
            pltpu.VMEM((devices * FIRST, 128), jnp.float32),
            pltpu.VMEM((devices * REST, 128), jnp.float32),
            jax.ShapeDtypeStruct((blocks,), jnp.int32),
        ),
        in_specs=[SMEM, SMEM] + [VMEM] * 5,
        out_specs=(VMEM, VMEM, SMEM),
        scratch_shapes=[pltpu.SMEM((devices,), jnp.int32)],
        name="pack",
    )(home, tile, forces, offsets, bx, by, bz)


def read_tiles(first_ref, tile_vmem, tile_smem, sem):
    devices = first_ref.shape[0] // FIRST
    lane = lax.broadcasted_iota(jnp.int32, (2, devices), 1)
    rank = lax.broadcasted_iota(jnp.int32, (2, devices), 0)
    found = jnp.full((2, devices), -1.0, jnp.float32)
    for d in range(devices):
        found = jnp.where(lane == d, first_ref[d * FIRST + 14 : d * FIRST + 16, :], found)
    tile = found.astype(jnp.int32)
    tile_vmem[...] = jnp.where(tile < 0, -1, (rank * devices + lane) * MARKS + tile)
    copy = pltpu.make_async_copy(tile_vmem, tile_smem, sem)
    copy.start()
    copy.wait()


def list_slots(tile_smem, rank, list_ref, start):
    def step(d, n):
        code = tile_smem[rank, d]
        list_ref[n] = code
        return n + 1 + lax.shift_right_arithmetic(code, 31)

    return lax.fori_loop(0, tile_smem.shape[1], step, start, unroll=16)


def pad_list(list_ref, end, spare):
    last = list_ref[jnp.maximum(end - 1, 0)]
    for extra in range(UNROLL - 1):
        list_ref[end + extra] = last if spare is None else spare
    list_ref[list_ref.shape[0] - 1] = (end + UNROLL - 1) // UNROLL


def weigh_slots(recv_ref, stride, weight_ref, first, devices):
    row = lax.broadcasted_iota(jnp.int32, (8, 128), 0)
    along_z = (row == 2) | (row == 5)

    def one(device):
        start = pl.multiple_of(device * stride, 8)
        off = recv_ref[pl.ds(start, 8), :]
        base = recv_ref[pl.ds(start + 8, 8), :]
        square = 1.0 + 4.0 * off - 4.0 * off * off
        rad = square * lax.rsqrt(square)
        low, high = 3.0 - 2.0 * off, 1.0 + 2.0 * off
        block = jnp.floor(base * 0.0625)
        to = pl.multiple_of((first + device) * WROWS, 8)
        weight_ref[pl.ds(to, 8), :] = jnp.where(along_z, base - 16.0 * block, base)
        weight_ref[pl.ds(to + 6, 1), :] = block[2:3, :]
        weight_ref[pl.ds(to + 7, 1), :] = block[5:6, :]
        weight_ref[pl.ds(to + 8, 8), :] = (low - rad) * 0.125
        weight_ref[pl.ds(to + 16, 8), :] = (low + rad) * 0.125
        weight_ref[pl.ds(to + 24, 8), :] = (high + rad) * 0.125
        weight_ref[pl.ds(to + 32, 8), :] = (high - rad) * 0.125

    def four(n, carry):
        for k in range(4):
            one(n * 4 + k)
        return carry

    lax.fori_loop(0, devices // 4, four, 0)


def wide(ref, row, dtype=jnp.float32):
    value = ref[pl.ds(row, 8, stride=0), :]
    if dtype == jnp.float32:
        return value
    return jnp.concatenate([value, value], axis=0).astype(dtype)


def picked(base, weights, cells):
    out = jnp.zeros(base.shape, base.dtype)
    for weight, cell in zip(weights, cells):
        out = jnp.where(base == cell, weight, out)
    return out


def cells_from(first, sublanes, dtype):
    cell = lax.broadcasted_iota(jnp.int32, (sublanes, 128), 0) + first
    return cell.astype(jnp.float32).astype(dtype)


def cell_table():
    f32, half = jnp.float32, jnp.bfloat16
    table = {(n, f32): cells_from(n, 8, f32) for n in range(-3, 9)}
    table.update({(n, half): cells_from(n, 16, half) for n in (-3, -2, -1, 0, 13, 14, 15)})
    return table


def weights_x(weight_ref, to, q, table):
    base = wide(weight_ref, to + q * 3)
    ws = [wide(weight_ref, to + 8 + 8 * m + q * 3) for m in range(4)]
    return [picked(base, ws, [table[8 * k - m, jnp.float32] for m in range(4)]) for k in range(TX // 8)]


def weights_y(weight_ref, to, q, table):
    base = wide(weight_ref, to + q * 3 + 1)
    ws = [wide(weight_ref, to + 8 + 8 * m + q * 3 + 1) for m in range(4)]
    return picked(base, ws, [table[-m, jnp.float32] for m in range(4)])


def weights_z(weight_ref, to, q, depth, table):
    half = jnp.bfloat16
    base = wide(weight_ref, to + q * 3 + 2, half)
    block = wide(weight_ref, to + 6 + q, half)
    ws = [wide(weight_ref, to + 8 + 8 * m + q * 3 + 2, half) for m in range(4)]
    low = picked(base, ws, [table[-m, half] for m in range(4)])
    high = picked(base, ws[1:], [table[16 - m, half] for m in range(1, 4)])
    zero = jnp.zeros((16, 128), half)
    here = [block == jnp.full((16, 128), k, half) for k in range(depth // 16)]
    out = []
    for k in range(depth // 16):
        before = jnp.where(here[k - 1], high, zero) if k else zero
        out.append(jnp.where(here[k], low, before))
    return out


def spread_blocks(list_ref, weight_ref, force_rows, acc_ref, wide_ref, tiles, depth):
    tile_rows = 3 * TX * TY

    def clear(n, carry):
        acc_ref[pl.ds(pl.multiple_of(n * tile_rows, 8), tile_rows), :] = jnp.zeros((tile_rows, depth), jnp.float32)
        return carry

    lax.fori_loop(0, tiles, clear, 0)
    table = cell_table()

    def build(slot, k):
        to = pl.multiple_of(slot * WROWS, 8)
        kernel_xy, weighted = [], []
        for q in range(2):
            wx = weights_x(weight_ref, to, q, table)
            at = (2 * k + q) * TX
            for part in range(TX // 8):
                wide_ref[at + part * 8 : at + part * 8 + 8, :] = wx[part]
            wy = weights_y(weight_ref, to, q, table)
            columns = [wide(wide_ref, at + i) * wy for i in range(TX)]
            kernel_xy.append(jnp.concatenate(columns, axis=0).astype(jnp.bfloat16))
            wz = weights_z(weight_ref, to, q, depth, table)
            parts = []
            for c in range(3):
                force = wide(*force_rows(slot, q * 3 + c), jnp.bfloat16)
                parts += [w * force for w in wz]
            weighted.append(jnp.concatenate(parts, axis=0))
        return lax.dot_general(
            jnp.concatenate(kernel_xy, axis=1),
            jnp.concatenate(weighted, axis=1),
            (((1,), (1,)), ((), ())),
            preferred_element_type=jnp.float32,
        )

    def add(tile, out):
        for c in range(3):
            here = pl.ds(pl.multiple_of(tile * tile_rows + c * TX * TY, 8), TX * TY)
            acc_ref[here, :] = acc_ref[here, :] + out[:, c * depth : (c + 1) * depth]

    def step(n, carry):
        codes = [list_ref[UNROLL * n + k] for k in range(UNROLL)]
        outs = [build(lax.shift_right_logical(code, MARK_BITS), k) for k, code in enumerate(codes)]
        for code, out in zip(codes, outs):
            add(code & (MARKS - 1), out)
        return carry

    lax.fori_loop(0, list_ref[list_ref.shape[0] - 1], step, 0)


def spread_first_kernel(
    first_ref, acc_hbm, weight_hbm, rest_ref, all_ref,
    acc_ref, weight_ref, wide_ref, list_ref, tile_vmem, tile_smem, sems, *, tiles
):
    devices = first_ref.shape[0] // FIRST
    read_tiles(first_ref, tile_vmem, tile_smem, sems.at[0])
    pad_list(list_ref, list_slots(tile_smem, 0, list_ref, 0), tiles)
    pad_list(rest_ref, list_slots(tile_smem, 1, rest_ref, 0), devices * MARKS + tiles)
    end = list_slots(tile_smem, 0, all_ref, 0)
    pad_list(all_ref, list_slots(tile_smem, 1, all_ref, end), None)
    weigh_slots(first_ref, FIRST, weight_ref, 0, devices)
    keep_weights = pltpu.make_async_copy(weight_ref, weight_hbm, sems.at[1])
    keep_weights.start()

    def force_rows(slot, idx):
        return first_ref, slot * FIRST + 16 + idx

    spread_blocks(list_ref, weight_ref, force_rows, acc_ref, wide_ref, tiles, acc_ref.shape[1])
    keep_acc = pltpu.make_async_copy(acc_ref, acc_hbm, sems.at[2])
    keep_acc.start()
    keep_weights.wait()
    keep_acc.wait()


def spread_rest_kernel(
    first_ref, rest_ref, list_ref, before_hbm, weight_first_hbm, velocity_hbm,
    forced_ref, weight_ref, xlo_ref, xhi_ref, ylo_ref, yhi_ref, velocity_ref, before_ref, acc_ref, wide_ref, sems,
):
    fetches = [
        pltpu.make_async_copy(velocity_hbm, velocity_ref, sems.at[0]),
        pltpu.make_async_copy(before_hbm, before_ref, sems.at[1]),
        pltpu.make_async_copy(weight_first_hbm, weight_ref.at[0 : weight_first_hbm.shape[0]], sems.at[2]),
    ]
    for fetch in fetches:
        fetch.start()
    depth = velocity_ref.shape[3]
    size_x, size_y = velocity_ref.shape[1:3]
    tiles_y = size_y // TY
    tiles = (size_x // TX) * tiles_y
    devices = first_ref.shape[0] // FIRST
    tile_rows = 3 * TX * TY
    weigh_slots(rest_ref, REST, weight_ref, devices, devices)

    def force_rows(slot, idx):
        device = slot - devices
        if idx < 2:
            return first_ref, device * FIRST + 6 + idx
        return rest_ref, device * REST + (6 if idx < 4 else 14) + idx % 2

    spread_blocks(list_ref, weight_ref, force_rows, acc_ref, wide_ref, tiles, depth)
    for fetch in fetches:
        fetch.wait()

    def finish(x, carry):
        for c in range(3):
            for ty in range(tiles_y):
                row = ((x // TX) * tiles_y + ty) * tile_rows + c * TX * TY + (x % TX) * TY
                here = (c, x, slice(ty * TY, (ty + 1) * TY), slice(None))
                rows = pl.ds(pl.multiple_of(row, 8), TY)
                value = velocity_ref[here] + time_step * (before_ref[rows, :] + acc_ref[rows, :])
                forced_ref[here] = value
                if ty == 0:
                    ylo_ref[c, pl.ds(x, 1), :] = value[0:1, :]
                if ty == tiles_y - 1:
                    yhi_ref[c, pl.ds(x, 1), :] = value[TY - 1 : TY, :]
        return carry

    lax.fori_loop(0, size_x, finish, 0, unroll=4)
    xlo_ref[...] = forced_ref[:, 0]
    xhi_ref[...] = forced_ref[:, size_x - 1]


def spread_params():
    return pltpu.CompilerParams(vmem_limit_bytes=20 << 20)


def spread_first(first, tiles, depth):
    devices = first.shape[0] // FIRST
    return pl.pallas_call(
        lambda *refs: spread_first_kernel(*refs, tiles=tiles),
        out_shape=(
            pltpu.HBM(((tiles + 1) * 3 * TX * TY, depth), jnp.float32),
            pltpu.HBM((devices * WROWS, 128), jnp.float32),
            jax.ShapeDtypeStruct((devices + LIST_SPARE,), jnp.int32),
            jax.ShapeDtypeStruct((2 * devices + LIST_SPARE,), jnp.int32),
        ),
        in_specs=[VMEM],
        out_specs=(HBM, HBM, SMEM, SMEM),
        scratch_shapes=[
            pltpu.VMEM(((tiles + 1) * 3 * TX * TY, depth), jnp.float32),
            pltpu.VMEM((devices * WROWS, 128), jnp.float32),
            pltpu.VMEM((2 * UNROLL * TX, 128), jnp.float32),
            pltpu.SMEM((devices + LIST_SPARE,), jnp.int32),
            pltpu.VMEM((2, devices), jnp.int32),
            pltpu.SMEM((2, devices), jnp.int32),
            pltpu.SemaphoreType.DMA((3,)),
        ],
        compiler_params=spread_params(),
        cost_estimate=pl.CostEstimate(flops=6 << 30, transcendentals=0, bytes_accessed=16 << 20),
        name="spread_first",
    )(first)


def spread_rest(first, rest, rest_list, before, weight_first, velocity):
    _, size_x, size_y, depth = velocity.shape
    devices = first.shape[0] // FIRST
    x_face = jax.ShapeDtypeStruct((3, size_y, depth), jnp.float32)
    y_face = jax.ShapeDtypeStruct((3, size_x, depth), jnp.float32)
    return pl.pallas_call(
        spread_rest_kernel,
        out_shape=(
            jax.ShapeDtypeStruct(velocity.shape, jnp.float32),
            jax.ShapeDtypeStruct((2 * devices * WROWS, 128), jnp.float32),
            x_face,
            x_face,
            y_face,
            y_face,
        ),
        in_specs=[VMEM, VMEM, SMEM, HBM, HBM, HBM],
        out_specs=(VMEM,) * 6,
        scratch_shapes=[
            pltpu.VMEM(velocity.shape, jnp.float32),
            pltpu.VMEM(before.shape, jnp.float32),
            pltpu.VMEM(before.shape, jnp.float32),
            pltpu.VMEM((2 * UNROLL * TX, 128), jnp.float32),
            pltpu.SemaphoreType.DMA((3,)),
        ],
        compiler_params=spread_params(),
        name="spread_rest",
    )(first, rest, rest_list, before, weight_first, velocity)


def sweep_kernel(
    list_ref, weight_ref, forced_ref, xlo_ref, xhi_ref, ylo_ref, yhi_ref, next_hbm, reply_ref,
    next_ref, pad_ref, tiled_ref, wide_ref, sem,
):
    _, size_x, size_y, depth = forced_ref.shape
    tiles_y = size_y // TY
    tiles = (size_x // TX) * tiles_y
    steps = list_ref[list_ref.shape[0] - 1]
    pad_ref[:, 1 : size_x + 1, 8 : size_y + 8, :] = forced_ref[...]
    pad_ref[:, 0, 8 : size_y + 8, :] = xlo_ref[...]
    pad_ref[:, size_x + 1, 8 : size_y + 8, :] = xhi_ref[...]
    pad_ref[:, 1 : size_x + 1, 7, :] = ylo_ref[...]
    pad_ref[:, 1 : size_x + 1, size_y + 8, :] = yhi_ref[...]
    lane = lax.broadcasted_iota(jnp.int32, (TY, depth), 1)
    first_lane, last_lane = lane == 0, lane == depth - 1

    def column(x2, carry):
        for ty in range(tiles_y):
            y0 = 8 + ty * TY
            halves = [[], [], []]
            for dx in range(2):
                x = x2 * 2 + dx + 1
                centre = [pad_ref[c, x, y0 : y0 + TY, :] for c in range(3)]
                drift = [(0.5 * time_step) * u for u in centre]
                ahead = [spread_rate - d for d in drift]
                behind = [spread_rate + d for d in drift]
                ahead[2] = jnp.where(last_lane, 0.0, ahead[2])
                behind[2] = jnp.where(first_lane, 0.0, behind[2])
                for c in range(3):
                    value = (
                        (1.0 - 6.0 * spread_rate) * centre[c]
                        + ahead[0] * pad_ref[c, x + 1, y0 : y0 + TY, :]
                        + behind[0] * pad_ref[c, x - 1, y0 : y0 + TY, :]
                        + ahead[1] * pad_ref[c, x, y0 + 1 : y0 + TY + 1, :]
                        + behind[1] * pad_ref[c, x, y0 - 1 : y0 + TY - 1, :]
                        + ahead[2] * pltpu.roll(centre[c], depth - 1, 1)
                        + behind[2] * pltpu.roll(centre[c], 1, 1)
                    )
                    next_ref[c, x - 1, ty * TY : (ty + 1) * TY, :] = value
                    halves[c].append(value)
            tile = (x2 // (TX // 2)) * tiles_y + ty
            for c in range(3):
                row = pl.multiple_of((tile * 3 + c) * (TX * TY) + (x2 % (TX // 2)) * 16, 16)
                tiled_ref[pl.ds(row, 16), :] = jnp.concatenate(halves[c], axis=0).astype(jnp.bfloat16)
        return carry

    lax.fori_loop(0, size_x // 2, column, 0)
    store = pltpu.make_async_copy(next_ref, next_hbm, sem)
    store.start()

    table = cell_table()

    def build(slot, mark, k):
        to = pl.multiple_of(slot * WROWS, 8)
        along_z = []
        for q in range(2):
            wx = weights_x(weight_ref, to, q, table)
            at = (2 * k + q) * TX
            for part in range(TX // 8):
                wide_ref[at + part * 8 : at + part * 8 + 8, :] = wx[part]
            along_z.append(jnp.concatenate(weights_z(weight_ref, to, q, depth, table), axis=0))
        row = pl.multiple_of(mark * (3 * TX * TY), 16)
        return lax.dot_general(
            tiled_ref[pl.ds(row, 3 * TX * TY), :],
            jnp.concatenate(along_z, axis=1),
            (((1,), (0,)), ((), ())),
            preferred_element_type=jnp.float32,
        )

    devices = weight_ref.shape[0] // (2 * WROWS)

    def finish(slot, along, k):
        to = pl.multiple_of(slot * WROWS, 8)
        rank = (slot >= devices).astype(jnp.int32)
        device = slot - rank * devices
        for q in range(2):
            at = (2 * k + q) * TX
            sums = [None] * 3
            for i in range(TX):
                weight = wide(wide_ref, at + i)
                for c in range(3):
                    row = c * TX * TY + i * TY
                    term = weight * along[row : row + TY, q * 128 : (q + 1) * 128]
                    sums[c] = term if sums[c] is None else sums[c] + term
            wy = weights_y(weight_ref, to, q, table)
            for c in range(3):
                result = jnp.sum(sums[c] * wy, axis=0, keepdims=True)
                reply_ref[device * 3 + c, pl.ds(2 * rank + q, 1), :] = result

    def step(n, carry):
        codes = [list_ref[UNROLL * n + k] for k in range(UNROLL)]
        outs = [build(lax.shift_right_logical(code, MARK_BITS), code & (MARKS - 1), k) for k, code in enumerate(codes)]
        for k, code in enumerate(codes):
            finish(lax.shift_right_logical(code, MARK_BITS), outs[k], k)
        return carry

    lax.fori_loop(0, steps, step, 0)
    store.wait()


def sweep(slot_list, weights, forced, xlo, xhi, ylo, yhi):
    smem = pl.BlockSpec(memory_space=pltpu.SMEM)
    vmem = pl.BlockSpec(memory_space=pltpu.VMEM)
    _, size_x, size_y, depth = forced.shape
    devices = weights.shape[0] // (2 * WROWS)
    return pl.pallas_call(
        sweep_kernel,
        out_shape=(
            jax.ShapeDtypeStruct(forced.shape, jnp.float32),
            jax.ShapeDtypeStruct((devices * 3, 4, 128), jnp.float32),
        ),
        in_specs=[smem] + [vmem] * 6,
        out_specs=(HBM, vmem),
        scratch_shapes=[
            pltpu.VMEM(forced.shape, jnp.float32),
            pltpu.VMEM((3, size_x + 2, size_y + 16, depth), jnp.float32),
            pltpu.VMEM((3 * size_x * size_y, depth), jnp.bfloat16),
            pltpu.VMEM((2 * UNROLL * TX, 128), jnp.float32),
            pltpu.SemaphoreType.DMA,
        ],
        compiler_params=pltpu.CompilerParams(vmem_limit_bytes=24 << 20),
        name="sweep",
    )(slot_list, weights, forced, xlo, xhi, ylo, yhi)


def gather_kernel(slot_ref, back_ref, out_ref):
    blocks = out_ref.shape[1]

    def take(group, carry):
        b0 = pl.multiple_of(group * 8, 8)
        slots = [slot_ref[b0 + j] for j in range(8)]
        for q in range(2):
            for c in range(3):
                rows = [back_ref[lax.shift_right_logical(slot, 1) * 3 + c, pl.ds((slot & 1) * 2 + q, 1), :] for slot in slots]
                out_ref[c, pl.ds(b0, 8), q * 128 : (q + 1) * 128] = jnp.concatenate(rows, axis=0)
        return carry

    lax.fori_loop(0, blocks // 8, take, 0)


def gather(slot, back):
    smem = pl.BlockSpec(memory_space=pltpu.SMEM)
    vmem = pl.BlockSpec(memory_space=pltpu.VMEM)
    return pl.pallas_call(
        gather_kernel,
        out_shape=jax.ShapeDtypeStruct((3, slot.shape[0], 256), jnp.float32),
        in_specs=[smem, vmem],
        out_specs=vmem,
        name="gather",
    )(slot, back)


def neighbour(value, axis, step):
    count = lax.axis_size(axis)
    return lax.ppermute(value, axis, [(i, i + step) for i in range(count) if 0 <= i + step < count])


def exchange(rows, devices):
    shaped = rows.reshape((devices, rows.shape[0] // devices) + rows.shape[1:])
    return lax.all_to_all(shaped, AXES, split_axis=0, concat_axis=0, tiled=True).reshape(rows.shape)


def body(velocity, forces, offsets, base_x, base_y, base_z, home_device, home_tile):
    devices = lax.axis_size("gx") * lax.axis_size("gy")
    _, size_x, size_y, depth = velocity.shape
    tiles = (size_x // TX) * (size_y // TY)
    send_first, send_rest, slot = pack(
        home_device[:, 0],
        home_tile,
        jnp.transpose(forces, (1, 0, 2)),
        jnp.transpose(offsets, (1, 0, 2)),
        base_x,
        base_y,
        base_z,
        devices,
    )
    first = exchange(send_first, devices)
    rest = exchange(send_rest, devices)
    before, weight_first, rest_list, all_list = spread_first(first, tiles, depth)
    before = pltpu.with_memory_space_constraint(before, pltpu.HBM)
    weight_first = pltpu.with_memory_space_constraint(weight_first, pltpu.HBM)
    velocity = pltpu.with_memory_space_constraint(velocity, pltpu.HBM)
    forced, weights, x_first, x_last, y_first, y_last = spread_rest(
        first, rest, rest_list, before, weight_first, velocity
    )
    xlo = neighbour(x_last, "gx", 1)
    xhi = neighbour(x_first, "gx", -1)
    ylo = neighbour(y_last, "gy", 1)
    yhi = neighbour(y_first, "gy", -1)
    velocity_next, reply = sweep(all_list, weights, forced, xlo, xhi, ylo, yhi)
    back = pltpu.with_memory_space_constraint(exchange(reply, devices), pltpu.VMEM)
    fibre = gather(slot, back)
    return velocity_next, jnp.transpose(fibre, (1, 0, 2))


def solution(mesh):
    return jax.shard_map(
        body,
        mesh=mesh,
        in_specs=(
            P(None, "gx", "gy", None),
            P(AXES, None, None),
            P(AXES, None, None),
            P(AXES, None),
            P(AXES, None),
            P(AXES, None),
            P(AXES, None),
            P(AXES),
        ),
        out_specs=(P(None, "gx", "gy", None), P(AXES, None, None)),
        check_vma=False,
    )
```
